32 devices in a mesh: prow: 4 (over y, x), pcol: 8 (over z, core).
Axes of the slice: x: 2, y: 2, z: 4, core: 2. Of those that a mesh axis runs over, the one named last changes fastest.
Arguments:
- known_inverse: bfloat16 [4096, 4, 8, 128], P('prow', None, 'pcol'), may hold values from -6 to 6
- pattern: int32 [32, 4, 8, 1], P('prow', None, 'pcol'), may hold values 0 or 1
- panel_one: bfloat16 [4096, 512], P(('prow', 'pcol')), may hold values from -0.09375 to 0.09375
- panel_two: bfloat16 [4096, 512], P(('prow', 'pcol')), may hold values from -0.09375 to 0.09375
- panel_top: bfloat16 [512, 512], replicated, may hold values from -0.25 to 0.25
- structure: int32 [4096], P(('prow', 'pcol')), may hold values from 0 to 1, as said below
- diag_one: bfloat16 [512, 512], replicated, may hold values from -6 to 6
- diag_two: bfloat16 [512, 512], replicated, may hold values from -6 to 6
Outputs:
- inverse_one: bfloat16 [4096, 512], P(('prow', 'pcol'))
- corner_one: bfloat16 [512, 512], replicated
- inverse_top: bfloat16 [512, 512], replicated
- inverse_two: bfloat16 [4096, 512], P(('prow', 'pcol'))
- corner_two: bfloat16 [512, 512], replicated
The draws below stay inside these ranges and needn't reach their ends.
Inputs may be any that keep to these rules, and one draw needn't show every extreme that they name: `structure`: in every aligned pair of rows (2 k and 2 k + 1) at least one entry is 1.
All inputs are finite; a program needn't handle non-finite values. No bound on the sum of `pattern` on one device may be relied on, other than what follows from the above.
Results may differ from the reference program's by a relative error of at most 0.0058.
Values may be sent and summed in bfloat16 or wider, within the bound.
No kernel may reach another device: no remote copies, remote signals or barrier semaphores. Data moves between devices by JAX's collectives and lax.ppermute only.
A program may use at most 128 MiB of HBM per device.

```python
import jax
import jax.numpy as jnp
from jax import lax

W = 512
BLK = 128
CB = 1
GRID_ROWS = 4
GRID_COLS = 8
C = 128
R = 4096
NB = 32


def draw_structure(key, part):
    choose = jax.random.randint(jax.random.fold_in(key, 71), (R // 2,), 0, 3)
    first = jnp.where(choose != 1, 1, 0)
    second = jnp.where(choose != 0, 1, 0)
    return jnp.stack([first, second], axis=1).reshape(R).astype(jnp.int32)


def place_ends(entries, stream_key, least, high):
    index_at = [jax.random.randint(jax.random.fold_in(stream_key, axis), (), 0, length) for axis, length in enumerate(entries.shape)]
    longest = entries.shape.index(max(entries.shape))
    neighbour = index_at[:longest] + [(index_at[longest] + 1) % entries.shape[longest]] + index_at[longest + 1:]
    return entries.at[tuple(index_at)].set(least).at[tuple(neighbour)].set(high)


def block_levels(rng, extent, shards, low, high):
    loudness, own = 1.0, jax.random.fold_in(rng, 6)
    for dim, parts in shards:
        heights = jnp.exp(jax.random.uniform(jax.random.fold_in(own, dim), (parts,), jnp.float32, low / len(shards), high / len(shards)))
        loudness = loudness * jnp.repeat(heights, extent[dim] // parts).reshape([-1 if axis == dim else 1 for axis in range(len(extent))])
    return loudness


def bell_draw(stream_key, extent, deviation, most, pieces=(), held_as=jnp.bfloat16):
    entries = deviation * jax.random.normal(stream_key, extent, jnp.float32)
    if pieces:
        entries = entries * block_levels(stream_key, extent, pieces, -0.22, 0.18)
    return jnp.clip(entries, -most, most).astype(held_as)


def setup_inputs(seed: int = 0) -> dict:
    arg_keys = jax.random.split(jax.random.key(seed), 9)
    known_inverse = bell_draw(arg_keys[0], (R, GRID_ROWS, GRID_COLS, C), 1.0, 6.0, ((0, 4), (2, 8)))
    pattern = place_ends((jax.random.randint(arg_keys[1], (NB, GRID_ROWS, GRID_COLS, CB), 0, 10) < 7).astype(jnp.int32), jax.random.fold_in(arg_keys[1], 1), 0, 1)
    panel_one = bell_draw(arg_keys[2], (R, W), R ** -0.5, 0.09375, ((0, 32),))
    panel_two = bell_draw(arg_keys[3], (R, W), R ** -0.5, 0.09375, ((0, 32),))
    panel_top = bell_draw(arg_keys[4], (W, W), W ** -0.5, 0.25)
    structure = draw_structure(jax.random.fold_in(arg_keys[8], 71), 0)
    diag_one = bell_draw(arg_keys[6], (W, W), 1.0, 6.0)
    diag_two = bell_draw(arg_keys[7], (W, W), 1.0, 6.0)
    return {"known_inverse": known_inverse, "pattern": pattern, "panel_one": panel_one, "panel_two": panel_two, "panel_top": panel_top, "structure": structure, "diag_one": diag_one, "diag_two": diag_two}


def masked_product(known_inverse, pattern, right_side):
    full_matrix = known_inverse.reshape(R, R)
    mark_table = pattern.reshape(NB, NB)
    group_blocks = NB // 16

    def one_group(group_index):
        row_block = lax.dynamic_slice_in_dim(full_matrix, (group_index * group_blocks * BLK).astype(jnp.int32), group_blocks * BLK, 0)
        flag_rows = lax.dynamic_slice_in_dim(mark_table, (group_index * group_blocks).astype(jnp.int32), group_blocks, 0)
        shaped = row_block.reshape(group_blocks, BLK, NB, BLK)
        kept_rows = jnp.where(flag_rows[:, None, :, None] > 0, shaped, jnp.zeros_like(shaped)).reshape(group_blocks * BLK, R)
        return jnp.dot(kept_rows, right_side, preferred_element_type=jnp.float32)

    stacked = lax.map(one_group, jnp.arange(16, dtype=jnp.int32))
    return stacked.reshape(R, right_side.shape[1])


def keep_rows(values, structure):
    return jnp.where(structure.reshape(R, 1) > 0, values, jnp.zeros_like(values))


def reference(known_inverse, pattern, panel_one, panel_two, panel_top, structure, diag_one, diag_two):
    masked_two = keep_rows(panel_two, structure)
    both_sums = masked_product(known_inverse, pattern, jnp.concatenate([panel_one, masked_two], axis=1))
    inverse_one = (-both_sums[:, :W]).astype(jnp.bfloat16)
    corner_full = diag_one.astype(jnp.float32) - jnp.dot(panel_one.T, inverse_one, preferred_element_type=jnp.float32)
    cross_sum = jnp.dot(inverse_one.T, masked_two, preferred_element_type=jnp.float32)
    top_value = jnp.dot(corner_full, panel_top.astype(jnp.float32), precision=lax.Precision.HIGHEST) + cross_sum
    inverse_top = (-top_value).astype(jnp.bfloat16)
    lower_two = -(both_sums[:, W:] + jnp.dot(inverse_one, panel_top, preferred_element_type=jnp.float32))
    inverse_two = keep_rows(lower_two, structure).astype(jnp.bfloat16)
    corner_two = diag_two.astype(jnp.float32) - jnp.dot(panel_top.T, inverse_top, preferred_element_type=jnp.float32) - jnp.dot(masked_two.T, inverse_two, preferred_element_type=jnp.float32)
    return inverse_one, corner_full.astype(jnp.bfloat16), inverse_top, inverse_two, corner_two.astype(jnp.bfloat16)
```

```python
import functools

import jax
import jax.numpy as jnp
from jax import lax
from jax.experimental import pallas as pl
from jax.experimental.pallas import tpu as pltpu
from jax.sharding import PartitionSpec as P

BLK = 128
BF = jnp.bfloat16
F32 = jnp.float32

SMEM = pl.BlockSpec(memory_space=pltpu.SMEM)
VMEM = pl.BlockSpec(memory_space=pltpu.VMEM)


def call(body, out, scratch, args, flops, name):
    size = sum(a.size * a.dtype.itemsize for a in args)
    return pl.pallas_call(
        body,
        out_shape=out,
        in_specs=[SMEM] + [VMEM] * (len(args) - 1),
        out_specs=[VMEM] * len(out),
        scratch_shapes=scratch,
        cost_estimate=pl.CostEstimate(flops=flops, bytes_accessed=size, transcendentals=0),
        compiler_params=pltpu.CompilerParams(vmem_limit_bytes=60 << 20),
        name=name,
    )(*args)


def sds(shape, dtype):
    return jax.ShapeDtypeStruct(shape, dtype)


def tree(parts):
    while len(parts) > 1:
        parts = [parts[k] + parts[k + 1] for k in range(0, len(parts), 2)]
    return parts[0]


def dot(a, b, dims=(1, 0)):
    return lax.dot_general(a, b, (((dims[0],), (dims[1],)), ((), ())), preferred_element_type=F32)


def product_body(n, nz, idx, mine, theirs, *refs):
    q, outs, (q_mine, q_theirs) = refs[:n], refs[n : n + nz], refs[n + nz :]
    p, z, c = idx[0], idx[1], idx[2]
    rows = q[0].shape[0] // 2
    for s in range(n):
        place = pl.ds(pl.multiple_of((p ^ s) * rows, rows), rows)
        q_mine[place, :] = q[s][:rows, :]
        q_theirs[place, :] = q[s][rows:, :]
    for s in range(nz):
        span = pl.ds(pl.multiple_of((z ^ s) * 2 * rows, 2 * rows), 2 * rows)
        value = dot(mine[span, :], q_mine[...]) + dot(theirs[span, :], q_theirs[...])
        for t in range(2):
            place = pl.ds(pl.multiple_of((c ^ t) * rows, rows), rows)
            outs[s][place, :] = value[t * rows : (t + 1) * rows].astype(outs[s].dtype)


def product(idx, mine, theirs, q, nz):
    n, shape = len(q), q[0].shape
    depth = mine.shape[1]
    out = [sds(shape, F32)] + [sds(shape, BF)] * (nz - 1)
    scratch = [pltpu.VMEM((depth, shape[1]), BF)] * 2
    return call(
        functools.partial(product_body, n, nz), out, scratch, [idx, mine, theirs, *q],
        4 * mine.shape[0] * depth * shape[1], "product",
    )


def first_body(n, nz, idx, *refs):
    parts, one_t, two = refs[:nz], refs[nz], refs[nz + 1]
    keep, give = refs[nz + 2 : nz + 4]
    outs, (own, cross) = refs[nz + 4 : nz + 4 + n], refs[nz + 4 + n :]
    p = idx[0]
    rows = keep.shape[0]
    value = tree([parts[s][...].astype(F32) for s in range(nz)])
    inverse = (-value).astype(BF)
    keep[...] = inverse[:rows]
    give[...] = inverse[rows:]
    own[...] = dot(one_t[...], inverse)
    cross[...] = dot(inverse, two[...], (0, 0))
    half = own.shape[1]
    tall, low = own.shape[0] // n, half // n
    for s in range(n):
        q = p ^ s
        kind = outs[s].dtype
        outs[s][:tall, :] = own[pl.ds(pl.multiple_of(q * tall, tall), tall), :].astype(kind)
        band = pl.ds(pl.multiple_of(q * low, low), low)
        outs[s][tall : tall + low, :] = cross[band, :half].astype(kind)
        outs[s][tall + low :, :] = cross[band, half:].astype(kind)


def first_sums(idx, parts, one_t, two, n):
    nz, (rows2, half) = len(parts), parts[0].shape
    width = one_t.shape[0]
    shard = (2 * width // n, half)
    out = [sds((rows2 // 2, half), BF)] * 2 + [sds(shard, F32)] + [sds(shard, BF)] * (n - 1)
    scratch = [pltpu.VMEM((width, half), F32), pltpu.VMEM((half, width), F32)]
    return call(
        functools.partial(first_body, n, nz), out, scratch, [idx, *parts, one_t, two],
        4 * width * rows2 * half, "first_sums",
    )


def second_body(n, nz, idx, *refs):
    parts, two_t = refs[:nz], refs[nz]
    keep, give = refs[nz + 1 : nz + 3]
    outs, (own,) = refs[nz + 3 : nz + 3 + n], refs[nz + 3 + n :]
    p = idx[0]
    rows = keep.shape[0]
    value = tree([parts[s][...].astype(F32) for s in range(nz)])
    keep[...] = value[:rows]
    give[...] = value[rows:]
    own[...] = dot(two_t[...], value.astype(BF))
    tall = own.shape[0] // n
    for s in range(n):
        place = pl.ds(pl.multiple_of((p ^ s) * tall, tall), tall)
        outs[s][...] = own[place, :].astype(outs[s].dtype)


def second_sums(idx, parts, two_t, n):
    nz, (rows2, half) = len(parts), parts[0].shape
    width = two_t.shape[0]
    shard = (width // n, half)
    out = [sds((rows2 // 2, half), F32)] * 2 + [sds(shard, F32)] + [sds(shard, BF)] * (n - 1)
    scratch = [pltpu.VMEM((width, half), F32)]
    return call(
        functools.partial(second_body, n, nz), out, scratch, [idx, *parts, two_t],
        2 * width * rows2 * half, "second_sums",
    )


def top_body(n, idx, *refs):
    mine, theirs = refs[:n], refs[n : 2 * n]
    top, top_t, start, one, two = refs[2 * n : 2 * n + 5]
    corner, inverse_top, rest, own, cross = refs[2 * n + 5 :]
    p, c = idx[0], idx[2]
    half = own.shape[2]
    tall, low = own.shape[1] // n, half // n
    for s in range(n):
        q = p ^ s
        high = pl.ds(pl.multiple_of(q * tall, tall), tall)
        band = pl.ds(pl.multiple_of(q * low, low), low)
        for source, t in ((mine[s], c), (theirs[s], 1 - c)):
            own[t, high, :] = source[:tall, :]
            cross[t, 0, band, :] = source[tall : tall + low, :]
            cross[t, 1, band, :] = source[tall + low :, :]
    for t in range(2):
        cols = slice(t * half, (t + 1) * half)
        corner[:, cols] = (one[:, cols].astype(F32) - own[t].astype(F32)).astype(BF)
    for t in range(2):
        cols = slice(t * half, (t + 1) * half)
        value = start[:, cols] - dot(own[0], top[:half, cols]) - dot(own[1], top[half:, cols])
        for k in range(2):
            rows = slice(k * half, (k + 1) * half)
            inverse_top[rows, cols] = (-(value[rows] + cross[k, t].astype(F32))).astype(BF)
    for t in range(2):
        rows = slice(t * half, (t + 1) * half)
        value = two[rows, :].astype(F32) - dot(top_t[rows, :], inverse_top[...])
        value = value + dot(cross[0, t], top[:half, :], (0, 0)) + dot(cross[1, t], top[half:, :], (0, 0))
        rest[rows, :] = value


def top_parts(idx, mine, theirs, top, top_t, start, one, two):
    n, width = len(mine), top.shape[0]
    half = width // 2
    out = [sds((width, width), BF), sds((width, width), BF), sds((width, width), F32)]
    scratch = [pltpu.VMEM((2, width, half), BF), pltpu.VMEM((2, 2, half, half), BF)]
    return call(
        functools.partial(top_body, n), out, scratch,
        [idx, *mine, *theirs, top, top_t, start, one, two], 6 * width**3, "top_parts",
    )


def last_body(n, idx, *refs):
    mine, theirs, rest, out = refs[:n], refs[n : 2 * n], refs[2 * n], refs[2 * n + 1]
    p, c = idx[0], idx[2]
    half = out.shape[1] // 2
    tall = out.shape[0] // n
    for s in range(n):
        high = pl.ds(pl.multiple_of((p ^ s) * tall, tall), tall)
        for source, t in ((mine[s], c), (theirs[s], 1 - c)):
            cols = pl.ds(pl.multiple_of(t * half, half), half)
            out[high, cols] = (rest[high, cols] + source[...].astype(F32)).astype(BF)


def last_part(idx, mine, theirs, rest):
    return call(
        functools.partial(last_body, len(mine)), [sds(rest.shape, BF)], [],
        [idx, *mine, *theirs, rest], 2 * rest.size, "last_part",
    )[0]


def on_device(
    n, m, known_inverse, pattern, panel_one, panel_two, panel_top, structure, diag_one, diag_two
):
    row_count = known_inverse.shape[0]
    col_groups = known_inverse.shape[1]
    piece_rows = known_inverse.shape[3]
    width = panel_one.shape[1]
    half = width // 2
    nz = m // 2
    block_rows = row_count // BLK
    piece_blocks = piece_rows // BLK
    p = lax.axis_index("prow")
    j = lax.axis_index("pcol")
    c = lax.rem(j, 2)
    idx = jnp.stack([p, j // 2, c]).astype(jnp.int32)
    swap = lambda x: lax.ppermute(x, "pcol", [(k, k ^ 1) for k in range(m)])
    over_z = lambda x, s: lax.ppermute(x, "pcol", [(k, k ^ (2 * s)) for k in range(m)])
    over_p = lambda x, s: lax.ppermute(x, "prow", [(k, k ^ s) for k in range(n)])

    row_flags = structure.reshape(piece_rows, 1) > 0
    masked_two = jnp.where(row_flags, panel_two, jnp.zeros_like(panel_two))
    both = jnp.concatenate((panel_one, masked_two), axis=1)
    chip = jnp.concatenate((both, swap(both)), axis=0)
    mine_one = jnp.where(c == 0, chip[:, :half], chip[:, half:width])
    mine_two = jnp.where(c == 0, chip[:, width : width + half], chip[:, width + half :])
    gathered_one = [mine_one] + [over_p(mine_one, s) for s in range(1, n)]
    gathered_two = [mine_two] + [over_p(mine_two, s) for s in range(1, n)]

    shaped = known_inverse.reshape(block_rows, BLK, col_groups, piece_blocks, BLK)
    flag_table = pattern.reshape(block_rows, 1, col_groups, piece_blocks, 1)
    masked = jnp.where(flag_table > 0, shaped, jnp.zeros_like(shaped)).reshape(
        row_count, col_groups * piece_rows
    )
    others = swap(masked)
    chip_one_t = chip[:, :width].T
    chip_two = chip[:, width:]
    chip_two_t = chip_two.T
    top_t = panel_top.T
    start = jnp.dot(diag_one, panel_top, preferred_element_type=F32)

    def exchange(parts):
        return [parts[0]] + [over_z(parts[s], s) for s in range(1, nz)]

    def total(parts):
        got = [parts[0]] + [over_p(parts[s], s).astype(F32) for s in range(1, n)]
        here = tree(got).astype(BF)
        got = [here] + [over_z(here, s) for s in range(1, nz)]
        here = tree([g.astype(F32) for g in got]).astype(BF)
        got = [here] + [over_p(here, s) for s in range(1, n)]
        return got, [swap(g) for g in got]

    parts_one = exchange(product(idx, masked, others, gathered_one, nz))
    parts_two = exchange(product(idx, masked, others, gathered_two, nz))
    keep_one, give_one, *sums_one = first_sums(idx, parts_one, chip_one_t, chip_two, n)
    keep_two, give_two, *sums_two = second_sums(idx, parts_two, chip_two_t, n)
    corner_one, inverse_top, rest = top_parts(
        idx, *total(sums_one), panel_top, top_t, start, diag_one, diag_two
    )
    corner_two = last_part(idx, *total(sums_two), rest)

    def whole_rows(keep, give):
        got = swap(give)
        return jnp.where(
            c == 0, jnp.concatenate((keep, got), axis=1), jnp.concatenate((got, keep), axis=1)
        )

    inverse_one = whole_rows(keep_one, give_one)
    lower_two = -(
        whole_rows(keep_two, give_two) + jnp.dot(inverse_one, panel_top, preferred_element_type=F32)
    )
    inverse_two = jnp.where(row_flags, lower_two, jnp.zeros_like(lower_two)).astype(BF)
    return inverse_one, corner_one, inverse_top, inverse_two, corner_two


def solution(mesh):
    in_specs = (
        P("prow", None, "pcol", None),
        P("prow", None, "pcol", None),
        P(("prow", "pcol"), None),
        P(("prow", "pcol"), None),
        P(),
        P(("prow", "pcol")),
        P(),
        P(),
    )
    out_specs = (P(("prow", "pcol"), None), P(), P(), P(("prow", "pcol"), None), P())
    return jax.shard_map(
        functools.partial(on_device, mesh.shape["prow"], mesh.shape["pcol"]),
        mesh=mesh, in_specs=in_specs, out_specs=out_specs, check_vma=False,
    )
```

```python
import functools
import math

import jax
import jax.numpy as jnp
from jax import lax
from jax.experimental import pallas as pl
from jax.experimental.pallas import tpu as pltpu
from jax.sharding import PartitionSpec as P

BLK = 128
BF = jnp.bfloat16
F32 = jnp.float32

VMEM = pl.BlockSpec(memory_space=pltpu.VMEM)


def sds(shape, dtype):
    return jax.ShapeDtypeStruct(shape, dtype)


def scratch(shape, dtype):
    return pltpu.VMEM(shape, dtype)


def call(body, out, temps, args, flops, name):
    size = lambda a: math.prod(a.shape) * jnp.dtype(a.dtype).itemsize
    held = sum(size(a) for a in (*args, *out))
    room = held + sum(size(t) for t in temps) + sum(2 * size(t) for t in out)
    return pl.pallas_call(
        body,
        out_shape=out,
        in_specs=[VMEM] * len(args),
        out_specs=[VMEM] * len(out),
        scratch_shapes=temps,
        cost_estimate=pl.CostEstimate(flops=flops, bytes_accessed=held, transcendentals=0),
        compiler_params=pltpu.CompilerParams(vmem_limit_bytes=room + (4 << 20)),
        name=name,
    )(*args)


def tree(parts):
    while len(parts) > 1:
        parts = [parts[k] + parts[k + 1] for k in range(0, len(parts), 2)]
    return parts[0]


def dot(a, b):
    return jnp.dot(a, b, preferred_element_type=F32)


def place():
    j = lax.axis_index("pcol")
    return lax.axis_index("prow"), j >> 1, j & 1


def block(index, size):
    return pl.ds(pl.multiple_of(index * size, size), size)


def pick_body(own, got, out):
    _, _, c = place()
    rows, half = own.shape[0], out.shape[1]
    out[:rows, :] = own[:, block(c, half)]
    out[rows:, :] = got[:, block(c, half)]


def pick(own, got):
    rows, width = own.shape
    return call(pick_body, [sds((2 * rows, width // 2), BF)], [], [own, got], 0, "pick")[0]


def turn_body(one, one_got, two, two_got, top, panels, top_t):
    rows, width = one.shape
    panels[:width, :rows] = one[...].T
    panels[:width, rows:] = one_got[...].T
    panels[width:, :rows] = two[...].T
    panels[width:, rows:] = two_got[...].T
    top_t[...] = top[...].T


def turn(one, one_got, two, two_got, top):
    rows, width = one.shape
    out = [sds((2 * width, 2 * rows), BF), sds(top.shape, BF)]
    return call(turn_body, out, [], [one, one_got, two, two_got, top], 0, "turn")


def product_body(n, nz, mine, theirs, *refs):
    q, outs, (q_mine, q_theirs) = refs[:n], refs[n : n + nz], refs[n + nz :]
    p, z, c = place()
    rows = q[0].shape[0] // 2
    for s in range(n):
        q_mine[block(p ^ s, rows), :] = q[s][:rows, :]
        q_theirs[block(p ^ s, rows), :] = q[s][rows:, :]
    for s in range(nz):
        span = block(z ^ s, 2 * rows)
        value = dot(mine[span, :], q_mine[...]) + dot(theirs[span, :], q_theirs[...])
        for t in range(2):
            outs[s][block(c ^ t, rows), :] = value[t * rows : (t + 1) * rows].astype(outs[s].dtype)


def product(mine, theirs, q, nz):
    n, shape = len(q), q[0].shape
    depth = mine.shape[1]
    out = [sds(shape, F32)] + [sds(shape, BF)] * (nz - 1)
    return call(
        functools.partial(product_body, n, nz), out, [scratch((depth, shape[1]), BF)] * 2,
        [mine, theirs, *q], 4 * mine.shape[0] * depth * shape[1], "product",
    )


def deal(p, source, first, outs):
    n = len(outs)
    tall = first // n
    for s in range(n):
        for k in range(source.shape[0] // first):
            rows = pl.ds(pl.multiple_of(k * first + (p ^ s) * tall, tall), tall)
            outs[s][k * tall : (k + 1) * tall, :] = source[rows, :].astype(outs[s].dtype)


def first_body(n, nz, *refs):
    parts, panels = refs[:nz], refs[nz]
    keep, give, outs, sums = refs[nz + 1], refs[nz + 2], refs[nz + 3 : nz + 3 + n], refs[nz + 3 + n]
    p, _, _ = place()
    rows = keep.shape[0]
    inverse = (-tree([parts[s][...].astype(F32) for s in range(nz)])).astype(BF)
    keep[...] = inverse[:rows]
    give[...] = inverse[rows:]
    sums[...] = dot(panels[...], inverse)
    deal(p, sums, sums.shape[0] // 2, outs)


def first_sums(parts, panels, n):
    nz, (rows2, half) = len(parts), parts[0].shape
    tall = panels.shape[0]
    shard = (tall // n, half)
    out = [sds((rows2 // 2, half), BF)] * 2 + [sds(shard, F32)] + [sds(shard, BF)] * (n - 1)
    return call(
        functools.partial(first_body, n, nz), out, [scratch((tall, half), F32)],
        [*parts, panels], 2 * tall * rows2 * half, "first_sums",
    )


def second_body(n, nz, *refs):
    parts, panels, give_one = refs[:nz], refs[nz], refs[nz + 1]
    keep, give, outs, sums = refs[nz + 2], refs[nz + 3], refs[nz + 4 : nz + 4 + n], refs[nz + 4 + n]
    p, _, _ = place()
    rows, half = keep.shape
    value = tree([parts[s][...].astype(F32) for s in range(nz)])
    keep[...] = value[:rows]
    give[:, :half] = give_one[...].astype(F32)
    give[:, half:] = value[rows:]
    width = sums.shape[0]
    sums[...] = dot(panels[width:, :], value.astype(BF))
    deal(p, sums, width, outs)


def second_sums(parts, panels, give_one, n):
    nz, (rows2, half) = len(parts), parts[0].shape
    width = panels.shape[0] // 2
    shard = (width // n, half)
    out = [sds((rows2 // 2, half), F32), sds((rows2 // 2, 2 * half), F32)]
    out += [sds(shard, F32)] + [sds(shard, BF)] * (n - 1)
    return call(
        functools.partial(second_body, n, nz), out, [scratch((width, half), F32)],
        [*parts, panels, give_one], 2 * width * rows2 * half, "second_sums",
    )


def top_body(n, *refs):
    mine, theirs = refs[:n], refs[n : 2 * n]
    top, top_t, one, two = refs[2 * n : 2 * n + 4]
    corner, inverse_top, rest, own, cross = refs[2 * n + 4 :]
    p, _, c = place()
    half = own.shape[1] // 2
    tall = own.shape[0] // n
    for s in range(n):
        for source, t in ((mine[s], c), (theirs[s], 1 - c)):
            own[block(p ^ s, tall), block(t, half)] = source[:tall, :]
            cross[block(p ^ s, tall), block(t, half)] = source[tall:, :]
    corner[...] = (one[...].astype(F32) - own[...].astype(F32)).astype(BF)
    value = dot(one[...], top[...]) - dot(own[...], top[...]) + cross[...].T.astype(F32)
    inverse_top[...] = (-value).astype(BF)
    rest[...] = (
        two[...].astype(F32) - dot(top_t[...], inverse_top[...]) + dot(cross[...], top[...])
    )


def top_parts(mine, theirs, top, top_t, one, two):
    n, shape = len(mine), top.shape
    out = [sds(shape, BF), sds(shape, BF), sds(shape, F32)]
    return call(
        functools.partial(top_body, n), out, [scratch(shape, BF)] * 2,
        [*mine, *theirs, top, top_t, one, two], 8 * shape[0] ** 3, "top_parts",
    )


def last_body(n, *refs):
    mine, theirs, rest, out = refs[:n], refs[n : 2 * n], refs[2 * n], refs[2 * n + 1]
    p, _, c = place()
    half = out.shape[1] // 2
    tall = out.shape[0] // n
    for s in range(n):
        for source, t in ((mine[s], c), (theirs[s], 1 - c)):
            at = (block(p ^ s, tall), block(t, half))
            out[at] = (rest[at] + source[...].astype(F32)).astype(BF)


def last_part(mine, theirs, rest):
    return call(
        functools.partial(last_body, len(mine)), [sds(rest.shape, BF)], [],
        [*mine, *theirs, rest], 2 * math.prod(rest.shape), "last_part",
    )[0]


def finish_body(keep_one, keep_two, got, top, flags, inverse_one, inverse_two, value):
    _, _, c = place()
    half = keep_one.shape[1]
    inverse_one[:, block(c, half)] = keep_one[...]
    inverse_one[:, block(1 - c, half)] = got[:, :half].astype(BF)
    value[:, block(c, half)] = keep_two[...]
    value[:, block(1 - c, half)] = got[:, half:]
    lower = -(value[...] + dot(inverse_one[...], top[...]))
    inverse_two[...] = jnp.where(flags[...] > 0, lower, jnp.zeros_like(lower)).astype(BF)


def finish(keep_one, keep_two, got, top, flags):
    shape = (keep_one.shape[0], top.shape[1])
    return call(
        finish_body, [sds(shape, BF)] * 2, [scratch(shape, F32)],
        [keep_one, keep_two, got, top, flags], 2 * shape[0] * top.shape[0] * shape[1], "finish",
    )


def on_device(
    n, m, known_inverse, pattern, panel_one, panel_two, panel_top, structure, diag_one, diag_two
):
    row_count = known_inverse.shape[0]
    col_groups = known_inverse.shape[1]
    piece_rows = known_inverse.shape[3]
    nz = m // 2
    block_rows = row_count // BLK
    piece_blocks = piece_rows // BLK
    swap = lambda x: lax.ppermute(x, "pcol", [(k, k ^ 1) for k in range(m)])
    over_z = lambda x, s: lax.ppermute(x, "pcol", [(k, k ^ (2 * s)) for k in range(m)])
    over_p = lambda x, s: lax.ppermute(x, "prow", [(k, k ^ s) for k in range(n)])

    flags = structure.reshape(piece_rows, 1)
    masked_two = jnp.where(flags > 0, panel_two, jnp.zeros_like(panel_two))
    got_one = swap(panel_one)
    got_two = swap(masked_two)
    mine_one = pick(panel_one, got_one)
    gathered_one = [mine_one] + [over_p(mine_one, s) for s in range(1, n)]
    mine_two = pick(masked_two, got_two)
    gathered_two = [mine_two] + [over_p(mine_two, s) for s in range(1, n)]
    panels, top_t = turn(panel_one, got_one, masked_two, got_two, panel_top)

    shaped = known_inverse.reshape(block_rows, BLK, col_groups, piece_blocks, BLK)
    flag_table = pattern.reshape(block_rows, 1, col_groups, piece_blocks, 1)
    masked = jnp.where(flag_table > 0, shaped, jnp.zeros_like(shaped)).reshape(
        row_count, col_groups * piece_rows
    )
    others = swap(masked)

    def exchange(parts):
        return [parts[0]] + [over_z(parts[s], s) for s in range(1, nz)]

    def total(parts):
        got = [parts[0]] + [over_p(parts[s], s).astype(F32) for s in range(1, n)]
        here = tree(got).astype(BF)
        got = [here] + [over_z(here, s) for s in range(1, nz)]
        here = tree([g.astype(F32) for g in got]).astype(BF)
        got = [here] + [over_p(here, s) for s in range(1, n)]
        return got, [swap(g) for g in got]

    parts_one = exchange(product(masked, others, gathered_one, nz))
    parts_two = exchange(product(masked, others, gathered_two, nz))
    keep_one, give_one, *sums_one = first_sums(parts_one, panels, n)
    keep_two, give, *sums_two = second_sums(parts_two, panels, give_one, n)
    corner_one, inverse_top, rest = top_parts(*total(sums_one), panel_top, top_t, diag_one, diag_two)
    corner_two = last_part(*total(sums_two), rest)
    inverse_one, inverse_two = finish(keep_one, keep_two, swap(give), panel_top, flags)
    return inverse_one, corner_one, inverse_top, inverse_two, corner_two


def solution(mesh):
    in_specs = (
        P("prow", None, "pcol", None),
        P("prow", None, "pcol", None),
        P(("prow", "pcol"), None),
        P(("prow", "pcol"), None),
        P(),
        P(("prow", "pcol")),
        P(),
        P(),
    )
    out_specs = (P(("prow", "pcol"), None), P(), P(), P(("prow", "pcol"), None), P())
    return jax.shard_map(
        functools.partial(on_device, mesh.shape["prow"], mesh.shape["pcol"]),
        mesh=mesh, in_specs=in_specs, out_specs=out_specs, check_vma=False,
    )
```

```python
import functools
import math

import jax
import jax.numpy as jnp
from jax import lax
from jax.experimental import pallas as pl
from jax.experimental.pallas import tpu as pltpu
from jax.sharding import PartitionSpec as P


BLK = 128
BF = jnp.bfloat16
F32 = jnp.float32

VMEM = pl.BlockSpec(memory_space=pltpu.VMEM)


def sds(shape, dtype):
    return jax.ShapeDtypeStruct(shape, dtype)


def scratch(shape, dtype):
    return pltpu.VMEM(shape, dtype)


def call(body, out, temps, args, flops):
    size = lambda a: math.prod(a.shape) * jnp.dtype(a.dtype).itemsize
    held = sum(size(a) for a in (*args, *out))
    room = held + sum(size(t) for t in temps) + sum(2 * size(t) for t in out)
    return pl.pallas_call(
        body,
        out_shape=out,
        in_specs=[VMEM] * len(args),
        out_specs=[VMEM] * len(out),
        scratch_shapes=temps,
        cost_estimate=pl.CostEstimate(flops=flops, bytes_accessed=held, transcendentals=0),
        compiler_params=pltpu.CompilerParams(vmem_limit_bytes=room + (4 << 20)),
    )(*args)


def tree(parts):
    while len(parts) > 1:
        parts = [parts[k] + parts[k + 1] for k in range(0, len(parts), 2)]
    return parts[0]


def dot(a, b):
    return jnp.dot(a, b, preferred_element_type=F32)


def place():
    j = lax.axis_index("pcol")
    return lax.axis_index("prow"), j >> 1, j & 1


def block(index, size):
    return pl.ds(pl.multiple_of(index * size, size), size)


def pick_body(own, got, out):
    _, _, c = place()
    rows, half = own.shape[0], out.shape[1]
    out[:rows, :] = own[:, block(c, half)]
    out[rows:, :] = got[:, block(c, half)]


def pick(own, got):
    rows, width = own.shape
    return call(pick_body, [sds((2 * rows, width // 2), BF)], [], [own, got], 0)[0]


def start_body(one, top, start, top_t):
    start[...] = dot(one[...], top[...])
    top_t[...] = top[...].T


def start_parts(one, top):
    out = [sds(top.shape, F32), sds(top.shape, BF)]
    return call(start_body, out, [], [one, top], 2 * top.shape[0] ** 3)


def product_body(n, nz, mine, theirs, *refs):
    q, outs, rhs = refs[:n], refs[n : n + nz], refs[n + nz]
    p, z, c = place()
    rows = q[0].shape[0] // 2
    depth = rhs.shape[0] // 2
    for s in range(n):
        rhs[block(p ^ s, rows), :] = q[s][:rows, :]
        rhs[pl.ds(pl.multiple_of(depth + (p ^ s) * rows, rows), rows), :] = q[s][rows:, :]
    for s in range(nz):
        span = block(z ^ s, 2 * rows)
        value = dot(mine[span, :], rhs[:depth, :]) + dot(theirs[span, :], rhs[depth:, :])
        for t in range(2):
            outs[s][block(c ^ t, rows), :] = value[t * rows : (t + 1) * rows].astype(outs[s].dtype)


def product(mine, theirs, q, nz):
    n, shape = len(q), q[0].shape
    depth = mine.shape[1]
    out = [sds(shape, F32)] + [sds(shape, BF)] * (nz - 1) + [sds((2 * depth, shape[1]), BF)]
    *parts, rhs = call(
        functools.partial(product_body, n, nz), out, [],
        [mine, theirs, *q], 4 * mine.shape[0] * depth * shape[1],
    )
    return parts, rhs


def first_body(n, nz, *refs):
    parts = refs[:nz]
    keep, give, outs, turned = refs[nz], refs[nz + 1], refs[nz + 2 : nz + 2 + n], refs[nz + 2 + n]
    p, _, _ = place()
    rows = keep.shape[0]
    inverse = -tree([parts[s][...].astype(F32) for s in range(nz)])
    keep[...] = inverse[:rows].astype(BF)
    give[...] = inverse[rows:].astype(BF)
    turned[...] = inverse.T
    for s in range(n):
        outs[s][...] = turned[block(p ^ s, outs[s].shape[0]), :].astype(BF)


def second_body(n, nz, *refs):
    parts, give_one = refs[:nz], refs[nz]
    keep, give, outs, turned = refs[nz + 1], refs[nz + 2], refs[nz + 3 : nz + 3 + n], refs[nz + 3 + n]
    p, _, _ = place()
    rows, half = keep.shape
    value = tree([parts[s][...].astype(F32) for s in range(nz)])
    keep[...] = value[:rows]
    give[:, :half] = give_one[...].astype(F32)
    give[:, half:] = value[rows:]
    turned[...] = value.T
    for s in range(n):
        outs[s][...] = turned[block(p ^ s, outs[s].shape[0]), :].astype(BF)


def first_turn(parts, n):
    nz, (rows2, half) = len(parts), parts[0].shape
    out = [sds((rows2 // 2, half), BF)] * 2 + [sds((half // n, rows2), BF)] * n
    return call(
        functools.partial(first_body, n, nz), out, [scratch((half, rows2), F32)],
        parts, nz * rows2 * half,
    )


def second_turn(parts, give_one, n):
    nz, (rows2, half) = len(parts), parts[0].shape
    out = [sds((rows2 // 2, half), F32), sds((rows2 // 2, 2 * half), F32)]
    out += [sds((half // n, rows2), BF)] * n
    return call(
        functools.partial(second_body, n, nz), out, [scratch((half, rows2), F32)],
        [*parts, give_one], nz * rows2 * half,
    )


def sums_body(n, *refs):
    pieces, panels, out, left = refs[:n], refs[n:-2], refs[-2], refs[-1]
    p, _, c = place()
    rows = pieces[0].shape[1] // 2
    depth, half = left.shape[1] // 2, panels[0].shape[1]
    for s in range(n):
        left[:, block(p ^ s, rows)] = pieces[s][:, :rows]
        left[:, pl.ds(pl.multiple_of(depth + (p ^ s) * rows, rows), rows)] = pieces[s][:, rows:]
    for k in range(len(panels) // 2):
        ours, got = panels[2 * k : 2 * k + 2]
        near = dot(left[...], ours[...])
        far = dot(left[:, :depth], got[depth:, :]) + dot(left[:, depth:], got[:depth, :])
        out[:, block(2 * k + c, half)] = near.astype(BF)
        out[:, block(2 * k + 1 - c, half)] = far.astype(BF)


def sums(pieces, panels):
    n, (low, _) = len(pieces), pieces[0].shape
    deep, half = panels[0].shape
    return call(
        functools.partial(sums_body, n), [sds((low, len(panels) * half), BF)], [scratch((low, deep), BF)],
        [*pieces, *panels], 2 * low * deep * half * len(panels),
    )[0]


def top_body(n, *refs):
    mine, theirs = refs[:n], refs[n : 2 * n]
    start, top, top_t, one, two = refs[2 * n : 2 * n + 5]
    corner, inverse_top, rest, own_t, cross = refs[2 * n + 5 :]
    p, _, c = place()
    low, width = mine[0].shape[0], own_t.shape[1]
    for s in range(n):
        for source, t in ((mine[s], c), (theirs[s], 1 - c)):
            rows = block(t * n + (p ^ s), low)
            own_t[rows, :] = source[:, :width]
            cross[rows, :] = source[:, width:]
    own = own_t[...].T
    corner[...] = (one[...].astype(F32) - own.astype(F32)).astype(BF)
    inverse_top[...] = (dot(own, top[...]) - start[...] - cross[...].astype(F32)).astype(BF)
    rest[...] = (
        two[...].astype(F32) - dot(top_t[...], inverse_top[...]) + dot(cross[...].T, top[...])
    )


def top_parts(mine, theirs, start, top, top_t, one, two):
    n, shape = len(mine), top.shape
    out = [sds(shape, BF), sds(shape, BF), sds(shape, F32)]
    return call(
        functools.partial(top_body, n), out, [scratch(shape, BF)] * 2,
        [*mine, *theirs, start, top, top_t, one, two], 6 * shape[0] ** 3,
    )


def last_body(n, *refs):
    mine, theirs, rest, out, tail_t = refs[:n], refs[n : 2 * n], *refs[2 * n :]
    p, _, c = place()
    low = mine[0].shape[0]
    for s in range(n):
        for source, t in ((mine[s], c), (theirs[s], 1 - c)):
            tail_t[block(t * n + (p ^ s), low), :] = source[...]
    out[...] = (rest[...] + tail_t[...].T.astype(F32)).astype(BF)


def last_part(mine, theirs, rest):
    return call(
        functools.partial(last_body, len(mine)), [sds(rest.shape, BF)], [scratch(rest.shape, BF)],
        [*mine, *theirs, rest], 2 * math.prod(rest.shape),
    )[0]


def finish_body(keep_one, keep_two, got, top, flags, inverse_one, inverse_two, value):
    _, _, c = place()
    half = keep_one.shape[1]
    inverse_one[:, block(c, half)] = keep_one[...]
    inverse_one[:, block(1 - c, half)] = got[:, :half].astype(BF)
    value[:, block(c, half)] = keep_two[...]
    value[:, block(1 - c, half)] = got[:, half:]
    lower = -(value[...] + dot(inverse_one[...], top[...]))
    inverse_two[...] = jnp.where(flags[...] > 0, lower, jnp.zeros_like(lower)).astype(BF)


def finish(keep_one, keep_two, got, top, flags):
    shape = (keep_one.shape[0], top.shape[1])
    return call(
        finish_body, [sds(shape, BF)] * 2, [scratch(shape, F32)],
        [keep_one, keep_two, got, top, flags], 2 * shape[0] * top.shape[0] * shape[1],
    )


def on_device(
    n, m, known_inverse, pattern, panel_one, panel_two, panel_top, structure, diag_one, diag_two
):
    row_count = known_inverse.shape[0]
    col_groups = known_inverse.shape[1]
    piece_rows = known_inverse.shape[3]
    nz = m // 2
    block_rows = row_count // BLK
    piece_blocks = piece_rows // BLK
    send = lambda x, axis, size, s: lax.ppermute(x, axis, [(k, k ^ s) for k in range(size)])
    swap = lambda x: send(x, "pcol", m, 1)
    over_z = lambda x, s: send(x, "pcol", m, 2 * s)
    over_p = lambda x, s: send(x, "prow", n, s)

    flags = structure.reshape(piece_rows, 1)
    masked_two = jnp.where(flags > 0, panel_two, jnp.zeros_like(panel_two))
    mine_one = pick(panel_one, swap(panel_one))
    mine_two = pick(masked_two, swap(masked_two))
    gather = lambda x: [x] + [over_p(x, s) for s in range(1, n)]
    gathered_one = gather(mine_one)
    gathered_two = gather(mine_two)

    shaped = known_inverse.reshape(block_rows, BLK, col_groups, piece_blocks, BLK)
    flag_table = pattern.reshape(block_rows, 1, col_groups, piece_blocks, 1)
    masked = jnp.where(flag_table > 0, shaped, jnp.zeros_like(shaped)).reshape(
        row_count, col_groups * piece_rows
    )
    others = swap(masked)
    start, top_t = start_parts(diag_one, panel_top)

    def exchange(parts):
        return [parts[0]] + [over_z(parts[s], s) for s in range(1, nz)]

    def spread(pieces):
        return [pieces[0]] + [over_p(pieces[s], s) for s in range(1, n)]

    def total(here):
        s = 1
        while s < nz:
            here = (here.astype(F32) + over_z(here, s).astype(F32)).astype(BF)
            s *= 2
        got = [here] + [over_p(here, s) for s in range(1, n)]
        return got, [swap(got[s]) for s in range(n)]

    parts_one, rows_one = product(masked, others, gathered_one, nz)
    parts_one = exchange(parts_one)
    parts_two, rows_two = product(masked, others, gathered_two, nz)
    parts_two = exchange(parts_two)
    panels = [rows_one, swap(rows_one), rows_two, swap(rows_two)]
    keep_one, give_one, *pieces_one = first_turn(parts_one, n)
    pieces_one = spread(pieces_one)
    keep_two, give, *pieces_two = second_turn(parts_two, give_one, n)
    pieces_two = spread(pieces_two)
    sums_one = sums(pieces_one, panels)
    sums_two = sums(pieces_two, panels[2:])
    corner_one, inverse_top, rest = top_parts(
        *total(sums_one), start, panel_top, top_t, diag_one, diag_two
    )
    corner_two = last_part(*total(sums_two), rest)
    inverse_one, inverse_two = finish(keep_one, keep_two, swap(give), panel_top, flags)
    return inverse_one, corner_one, inverse_top, inverse_two, corner_two


def solution(mesh):
    in_specs = (
        P("prow", None, "pcol", None),
        P("prow", None, "pcol", None),
        P(("prow", "pcol"), None),
        P(("prow", "pcol"), None),
        P(),
        P(("prow", "pcol")),
        P(),
        P(),
    )
    out_specs = (P(("prow", "pcol"), None), P(), P(), P(("prow", "pcol"), None), P())
    n, m = mesh.shape["prow"], mesh.shape["pcol"]

    def body(*args):
        return on_device(n, m, *args)

    return jax.shard_map(body, mesh=mesh, in_specs=in_specs, out_specs=out_specs, check_vma=False)
```

```python
import functools
import math

import jax
import jax.numpy as jnp
from jax import lax
from jax.experimental import pallas as pl
from jax.experimental.pallas import tpu as pltpu
from jax.sharding import PartitionSpec as P


BLK = 128
BF = jnp.bfloat16
F32 = jnp.float32

VMEM = pl.BlockSpec(memory_space=pltpu.VMEM)


def sds(shape, dtype):
    return jax.ShapeDtypeStruct(shape, dtype)


def scratch(shape, dtype):
    return pltpu.VMEM(shape, dtype)


def call(body, out, temps, args, flops):
    size = lambda a: math.prod(a.shape) * jnp.dtype(a.dtype).itemsize
    held = sum(size(a) for a in (*args, *out))
    room = held + sum(size(t) for t in temps) + sum(2 * size(t) for t in out)
    return pl.pallas_call(
        body,
        out_shape=out,
        in_specs=[VMEM] * len(args),
        out_specs=[VMEM] * len(out),
        scratch_shapes=temps,
        cost_estimate=pl.CostEstimate(flops=flops, bytes_accessed=held, transcendentals=0),
        compiler_params=pltpu.CompilerParams(vmem_limit_bytes=room + (4 << 20)),
    )(*args)


def tree(parts):
    while len(parts) > 1:
        parts = [parts[k] + parts[k + 1] for k in range(0, len(parts), 2)]
    return parts[0]


def dot(a, b):
    return jnp.dot(a, b, preferred_element_type=F32)


def place():
    j = lax.axis_index("pcol")
    return lax.axis_index("prow"), j >> 1, j & 1


def block(index, size):
    return pl.ds(pl.multiple_of(index * size, size), size)


def pick_body(own, got, out):
    _, _, c = place()
    rows, half = own.shape[0], out.shape[1]
    out[:rows, :] = own[:, block(c, half)]
    out[rows:, :] = got[:, block(c, half)]


def pick(own, got):
    rows, width = own.shape
    return call(pick_body, [sds((2 * rows, width // 2), BF)], [], [own, got], 0)[0]


def start_body(one, top, start, top_t):
    start[...] = dot(one[...], top[...])
    top_t[...] = top[...].T


def start_parts(one, top):
    out = [sds(top.shape, F32), sds(top.shape, BF)]
    return call(start_body, out, [], [one, top], 2 * top.shape[0] ** 3)


def sequence(nz):
    if nz == 1:
        return [0]
    stay = [2 * k for k in sequence(nz // 2)]
    return stay + [k ^ 1 for k in stay]


def product_body(n, nz, mine, theirs, *refs):
    q, (stay, leave, rhs) = refs[:n], refs[n:]
    p, z, c = place()
    rows = q[0].shape[0] // 2
    depth = rhs.shape[0] // 2
    for s in range(n):
        rhs[block(p ^ s, rows), :] = q[s][:rows, :]
        rhs[pl.ds(pl.multiple_of(depth + (p ^ s) * rows, rows), rows), :] = q[s][rows:, :]
    order = sequence(nz)
    for k in range(nz // 2, nz):
        emit(leave, k - nz // 2, order[k], z, c, rows, mine, theirs, rhs)
    for k in range(nz // 2):
        emit(stay, k, order[k], z, c, rows, mine, theirs, rhs)


def emit(out, k, offset, z, c, rows, mine, theirs, rhs):
    depth = rhs.shape[0] // 2
    span = block(z ^ offset, 2 * rows)
    value = dot(mine[span, :], rhs[:depth, :]) + dot(theirs[span, :], rhs[depth:, :])
    for t in range(2):
        out[block(2 * k + (c ^ t), rows), :] = value[t * rows : (t + 1) * rows].astype(out.dtype)


def product(mine, theirs, q, nz):
    n, (rows, half) = len(q), q[0].shape
    depth = mine.shape[1]
    shape = (nz // 2 * rows, half)
    out = [sds(shape, F32), sds(shape, BF), sds((2 * depth, half), BF)]
    return call(
        functools.partial(product_body, n, nz), out, [],
        [mine, theirs, *q], 4 * mine.shape[0] * depth * half,
    )


def fold_body(held, got, stay, leave):
    rows = stay.shape[0]
    stay[...] = held[:rows] + got[:rows].astype(F32)
    leave[...] = (held[rows:] + got[rows:].astype(F32)).astype(BF)


def fold(held, got):
    shape = (held.shape[0] // 2, held.shape[1])
    return call(fold_body, [sds(shape, F32), sds(shape, BF)], [], [held, got], 2 * held.size)


def first_body(n, nz, *refs):
    parts = refs[:nz]
    keep, give, outs, turned = refs[nz], refs[nz + 1], refs[nz + 2 : nz + 2 + n], refs[nz + 2 + n]
    p, _, _ = place()
    rows = keep.shape[0]
    inverse = -tree([parts[s][...].astype(F32) for s in range(nz)])
    keep[...] = inverse[:rows].astype(BF)
    give[...] = inverse[rows:].astype(BF)
    turned[...] = inverse.T
    for s in range(n):
        outs[s][...] = turned[block(p ^ s, outs[s].shape[0]), :].astype(BF)


def second_body(n, nz, *refs):
    parts, give_one = refs[:nz], refs[nz]
    keep, give, outs, turned = refs[nz + 1], refs[nz + 2], refs[nz + 3 : nz + 3 + n], refs[nz + 3 + n]
    p, _, _ = place()
    rows, half = keep.shape
    value = tree([parts[s][...].astype(F32) for s in range(nz)])
    keep[...] = value[:rows]
    give[:, :half] = give_one[...].astype(F32)
    give[:, half:] = value[rows:]
    turned[...] = value.T
    for s in range(n):
        outs[s][...] = turned[block(p ^ s, outs[s].shape[0]), :].astype(BF)


def first_turn(parts, n):
    nz, (rows2, half) = len(parts), parts[0].shape
    out = [sds((rows2 // 2, half), BF)] * 2 + [sds((half // n, rows2), BF)] * n
    return call(
        functools.partial(first_body, n, nz), out, [scratch((half, rows2), F32)],
        parts, nz * rows2 * half,
    )


def second_turn(parts, give_one, n):
    nz, (rows2, half) = len(parts), parts[0].shape
    out = [sds((rows2 // 2, half), F32), sds((rows2 // 2, 2 * half), F32)]
    out += [sds((half // n, rows2), BF)] * n
    return call(
        functools.partial(second_body, n, nz), out, [scratch((half, rows2), F32)],
        [*parts, give_one], nz * rows2 * half,
    )


def sums_body(n, *refs):
    pieces, panels, out, left = refs[:n], refs[n:-2], refs[-2], refs[-1]
    p, _, c = place()
    rows = pieces[0].shape[1] // 2
    depth, half = left.shape[1] // 2, panels[0].shape[1]
    for s in range(n):
        left[:, block(p ^ s, rows)] = pieces[s][:, :rows]
        left[:, pl.ds(pl.multiple_of(depth + (p ^ s) * rows, rows), rows)] = pieces[s][:, rows:]
    for k in range(len(panels) // 2):
        ours, got = panels[2 * k : 2 * k + 2]
        near = dot(left[...], ours[...])
        far = dot(left[:, :depth], got[depth:, :]) + dot(left[:, depth:], got[:depth, :])
        out[:, block(2 * k + c, half)] = near.astype(BF)
        out[:, block(2 * k + 1 - c, half)] = far.astype(BF)


def sums(pieces, panels):
    n, (low, _) = len(pieces), pieces[0].shape
    deep, half = panels[0].shape
    return call(
        functools.partial(sums_body, n), [sds((low, len(panels) * half), BF)], [scratch((low, deep), BF)],
        [*pieces, *panels], 2 * low * deep * half * len(panels),
    )[0]


def top_body(n, *refs):
    mine, theirs = refs[:n], refs[n : 2 * n]
    start, top, top_t, one, two = refs[2 * n : 2 * n + 5]
    corner, inverse_top, rest, own_t, cross = refs[2 * n + 5 :]
    p, _, c = place()
    low, width = mine[0].shape[0], own_t.shape[1]
    for s in range(n):
        for source, t in ((mine[s], c), (theirs[s], 1 - c)):
            rows = block(t * n + (p ^ s), low)
            own_t[rows, :] = source[:, :width]
            cross[rows, :] = source[:, width:]
    own = own_t[...].T
    corner[...] = (one[...].astype(F32) - own.astype(F32)).astype(BF)
    inverse_top[...] = (dot(own, top[...]) - start[...] - cross[...].astype(F32)).astype(BF)
    rest[...] = (
        two[...].astype(F32) - dot(top_t[...], inverse_top[...]) + dot(cross[...].T, top[...])
    )


def top_parts(mine, theirs, start, top, top_t, one, two):
    n, shape = len(mine), top.shape
    out = [sds(shape, BF), sds(shape, BF), sds(shape, F32)]
    return call(
        functools.partial(top_body, n), out, [scratch(shape, BF)] * 2,
        [*mine, *theirs, start, top, top_t, one, two], 6 * shape[0] ** 3,
    )


def last_body(n, *refs):
    mine, theirs, rest, out, tail_t = refs[:n], refs[n : 2 * n], *refs[2 * n :]
    p, _, c = place()
    low = mine[0].shape[0]
    for s in range(n):
        for source, t in ((mine[s], c), (theirs[s], 1 - c)):
            tail_t[block(t * n + (p ^ s), low), :] = source[...]
    out[...] = (rest[...] + tail_t[...].T.astype(F32)).astype(BF)


def last_part(mine, theirs, rest):
    return call(
        functools.partial(last_body, len(mine)), [sds(rest.shape, BF)], [scratch(rest.shape, BF)],
        [*mine, *theirs, rest], 2 * math.prod(rest.shape),
    )[0]


def finish_body(keep_one, keep_two, got, top, flags, inverse_one, inverse_two, value):
    _, _, c = place()
    half = keep_one.shape[1]
    inverse_one[:, block(c, half)] = keep_one[...]
    inverse_one[:, block(1 - c, half)] = got[:, :half].astype(BF)
    value[:, block(c, half)] = keep_two[...]
    value[:, block(1 - c, half)] = got[:, half:]
    lower = -(value[...] + dot(inverse_one[...], top[...]))
    inverse_two[...] = jnp.where(flags[...] > 0, lower, jnp.zeros_like(lower)).astype(BF)


def finish(keep_one, keep_two, got, top, flags):
    shape = (keep_one.shape[0], top.shape[1])
    return call(
        finish_body, [sds(shape, BF)] * 2, [scratch(shape, F32)],
        [keep_one, keep_two, got, top, flags], 2 * shape[0] * top.shape[0] * shape[1],
    )


def on_device(
    n, m, known_inverse, pattern, panel_one, panel_two, panel_top, structure, diag_one, diag_two
):
    row_count = known_inverse.shape[0]
    col_groups = known_inverse.shape[1]
    piece_rows = known_inverse.shape[3]
    nz = m // 2
    block_rows = row_count // BLK
    piece_blocks = piece_rows // BLK
    send = lambda x, axis, size, s: lax.ppermute(x, axis, [(k, k ^ s) for k in range(size)])
    swap = lambda x: send(x, "pcol", m, 1)
    over_z = lambda x, s: send(x, "pcol", m, 2 * s)
    over_p = lambda x, s: send(x, "prow", n, s)

    flags = structure.reshape(piece_rows, 1)
    masked_two = jnp.where(flags > 0, panel_two, jnp.zeros_like(panel_two))
    mine_one = pick(panel_one, swap(panel_one))
    mine_two = pick(masked_two, swap(masked_two))
    gather = lambda x: [x] + [over_p(x, s) for s in range(1, n)]
    gathered_one = gather(mine_one)
    gathered_two = gather(mine_two)

    shaped = known_inverse.reshape(block_rows, BLK, col_groups, piece_blocks, BLK)
    flag_table = pattern.reshape(block_rows, 1, col_groups, piece_blocks, 1)
    masked = jnp.where(flag_table > 0, shaped, jnp.zeros_like(shaped)).reshape(
        row_count, col_groups * piece_rows
    )
    others = swap(masked)
    start, top_t = start_parts(diag_one, panel_top)

    def exchange(stay, leave):
        got, s = over_z(leave, 1), 2
        while s < nz:
            stay, leave = fold(stay, got)
            got, s = over_z(leave, s), 2 * s
        return [stay, got]

    def spread(pieces):
        return [pieces[0]] + [over_p(pieces[s], s) for s in range(1, n)]

    def total(here):
        s = 1
        while s < nz:
            here = (here.astype(F32) + over_z(here, s).astype(F32)).astype(BF)
            s *= 2
        got = [here] + [over_p(here, s) for s in range(1, n)]
        return got, [swap(got[s]) for s in range(n)]

    *parts_one, rows_one = product(masked, others, gathered_one, nz)
    parts_one = exchange(*parts_one)
    *parts_two, rows_two = product(masked, others, gathered_two, nz)
    parts_two = exchange(*parts_two)
    panels = [rows_one, swap(rows_one), rows_two, swap(rows_two)]
    keep_one, give_one, *pieces_one = first_turn(parts_one, n)
    pieces_one = spread(pieces_one)
    keep_two, give, *pieces_two = second_turn(parts_two, give_one, n)
    pieces_two = spread(pieces_two)
    sums_one = sums(pieces_one, panels)
    sums_two = sums(pieces_two, panels[2:])
    corner_one, inverse_top, rest = top_parts(
        *total(sums_one), start, panel_top, top_t, diag_one, diag_two
    )
    corner_two = last_part(*total(sums_two), rest)
    inverse_one, inverse_two = finish(keep_one, keep_two, swap(give), panel_top, flags)
    return inverse_one, corner_one, inverse_top, inverse_two, corner_two


def solution(mesh):
    in_specs = (
        P("prow", None, "pcol", None),
        P("prow", None, "pcol", None),
        P(("prow", "pcol"), None),
        P(("prow", "pcol"), None),
        P(),
        P(("prow", "pcol")),
        P(),
        P(),
    )
    out_specs = (P(("prow", "pcol"), None), P(), P(), P(("prow", "pcol"), None), P())
    n, m = mesh.shape["prow"], mesh.shape["pcol"]

    def body(*args):
        return on_device(n, m, *args)

    return jax.shard_map(body, mesh=mesh, in_specs=in_specs, out_specs=out_specs, check_vma=False)
```

```python
import functools
import math

import jax
import jax.numpy as jnp
from jax import lax
from jax.experimental import pallas as pl
from jax.experimental.pallas import tpu as pltpu
from jax.sharding import PartitionSpec as P


BLK = 128
BF = jnp.bfloat16
F32 = jnp.float32

VMEM = pl.BlockSpec(memory_space=pltpu.VMEM)


def sds(shape, dtype):
    return jax.ShapeDtypeStruct(shape, dtype)


def scratch(shape, dtype):
    return pltpu.VMEM(shape, dtype)


def call(body, out, temps, args, flops):
    size = lambda a: math.prod(a.shape) * jnp.dtype(a.dtype).itemsize
    held = sum(size(a) for a in (*args, *out))
    room = held + sum(size(t) for t in temps) + sum(2 * size(t) for t in out)
    return pl.pallas_call(
        body,
        out_shape=out,
        in_specs=[VMEM] * len(args),
        out_specs=[VMEM] * len(out),
        scratch_shapes=temps,
        cost_estimate=pl.CostEstimate(flops=flops, bytes_accessed=held, transcendentals=0),
        compiler_params=pltpu.CompilerParams(vmem_limit_bytes=room + (4 << 20)),
    )(*args)


def tree(parts):
    while len(parts) > 1:
        parts = [parts[k] + parts[k + 1] for k in range(0, len(parts), 2)]
    return parts[0]


def dot(a, b):
    return jnp.dot(a, b, preferred_element_type=F32)


def place():
    j = lax.axis_index("pcol")
    return lax.axis_index("prow"), j >> 1, j & 1


def block(index, size):
    return pl.ds(pl.multiple_of(index * size, size), size)


def pick_body(own, got, out):
    _, _, c = place()
    rows, half = own.shape[0], out.shape[1]
    out[:rows, :] = own[:, block(c, half)]
    out[rows:, :] = got[:, block(c, half)]


def pick(own, got):
    rows, width = own.shape
    return call(pick_body, [sds((2 * rows, width // 2), BF)], [], [own, got], 0)[0]


def split_body(own, near, far):
    _, _, c = place()
    half = near.shape[1]
    near[...] = own[:, block(c, half)]
    far[...] = own[:, block(1 - c, half)]


def split(own):
    shape = (own.shape[0], own.shape[1] // 2)
    return call(split_body, [sds(shape, BF)] * 2, [], [own], 0)


def kept_rows(flags, values):
    rows = values.shape[0]
    mask = jnp.broadcast_to(flags.astype(F32), (rows, rows)).T > 0
    mask = jnp.concatenate([mask.astype(F32)] * (values.shape[1] // rows), axis=1)
    return jnp.where(mask > 0, values, jnp.zeros_like(values))


def keep_body(flags, values, out):
    out[...] = kept_rows(flags[...], values[...].astype(F32)).astype(BF)


def keep(flags, values):
    return call(keep_body, [sds(values.shape, BF)], [], [flags, values], values.size)[0]


def add_body(one, two, out):
    out[...] = (one[...].astype(F32) + two[...].astype(F32)).astype(out.dtype)


def add(one, two):
    return call(add_body, [sds(one.shape, BF)], [], [one, two], one.size)[0]


def start_body(one, top, start, top_t):
    start[...] = dot(one[...], top[...])
    top_t[...] = top[...].T


def start_parts(one, top):
    out = [sds(top.shape, F32), sds(top.shape, BF)]
    return call(start_body, out, [], [one, top], 2 * top.shape[0] ** 3)


def sequence(nz):
    if nz == 1:
        return [0]
    stay = [2 * k for k in sequence(nz // 2)]
    return stay + [k ^ 1 for k in stay]


def product_body(n, nz, mine, theirs, *refs):
    near, far, (stay, leave, rhs) = refs[:n], refs[n:-3], refs[-3:]
    p, z, c = place()
    depth = rhs.shape[0] // 2
    rows = depth // n
    for s in range(n):
        other = far[s][...] if far else near[s][rows:, :]
        rhs[block(p ^ s, rows), :] = near[s][:rows, :]
        rhs[pl.ds(pl.multiple_of(depth + (p ^ s) * rows, rows), rows), :] = other
    order = sequence(nz)
    for k in range(nz // 2, nz):
        emit(leave, k - nz // 2, order[k], z, c, rows, mine, theirs, rhs)
    for k in range(nz // 2):
        emit(stay, k, order[k], z, c, rows, mine, theirs, rhs)


def emit(out, k, offset, z, c, rows, mine, theirs, rhs):
    depth = rhs.shape[0] // 2
    span = block(z ^ offset, 2 * rows)
    value = dot(mine[span, :], rhs[:depth, :]) + dot(theirs[span, :], rhs[depth:, :])
    for t in range(2):
        out[block(2 * k + (c ^ t), rows), :] = value[t * rows : (t + 1) * rows].astype(out.dtype)


def product(mine, theirs, near, far, nz):
    n, half = len(near), near[0].shape[1]
    depth = mine.shape[1]
    rows = 2 * depth // n
    shape = (nz // 2 * rows, half)
    out = [sds(shape, F32), sds(shape, BF), sds((2 * depth, half), BF)]
    return call(
        functools.partial(product_body, n, nz), out, [],
        [mine, theirs, *near, *far], 4 * mine.shape[0] * depth * half,
    )


def fold_body(held, got, stay, leave):
    rows = stay.shape[0]
    stay[...] = held[:rows] + got[:rows].astype(F32)
    leave[...] = (held[rows:] + got[rows:].astype(F32)).astype(BF)


def fold(held, got):
    shape = (held.shape[0] // 2, held.shape[1])
    return call(fold_body, [sds(shape, F32), sds(shape, BF)], [], [held, got], 2 * held.size)


def first_body(n, nz, *refs):
    parts = refs[:nz]
    keep, give, outs, turned = refs[nz], refs[nz + 1], refs[nz + 2 : nz + 2 + n], refs[nz + 2 + n]
    p, _, _ = place()
    rows = keep.shape[0]
    inverse = -tree([parts[s][...].astype(F32) for s in range(nz)])
    keep[...] = inverse[:rows].astype(BF)
    give[...] = inverse[rows:].astype(BF)
    turned[...] = inverse.T
    for s in range(n):
        outs[s][...] = turned[block(p ^ s, outs[s].shape[0]), :].astype(BF)


def second_body(n, nz, *refs):
    parts, give_one = refs[:nz], refs[nz]
    keep, give, outs, turned = refs[nz + 1], refs[nz + 2], refs[nz + 3 : nz + 3 + n], refs[nz + 3 + n]
    p, _, _ = place()
    rows, half = keep.shape
    value = tree([parts[s][...].astype(F32) for s in range(nz)])
    keep[...] = value[:rows]
    give[:, :half] = give_one[...].astype(F32)
    give[:, half:] = value[rows:]
    turned[...] = value.T
    for s in range(n):
        outs[s][...] = turned[block(p ^ s, outs[s].shape[0]), :].astype(BF)


def first_turn(parts, n):
    nz, (rows2, half) = len(parts), parts[0].shape
    out = [sds((rows2 // 2, half), BF)] * 2 + [sds((half // n, rows2), BF)] * n
    return call(
        functools.partial(first_body, n, nz), out, [scratch((half, rows2), F32)],
        parts, nz * rows2 * half,
    )


def second_turn(parts, give_one, n):
    nz, (rows2, half) = len(parts), parts[0].shape
    out = [sds((rows2 // 2, half), F32), sds((rows2 // 2, 2 * half), F32)]
    out += [sds((half // n, rows2), BF)] * n
    return call(
        functools.partial(second_body, n, nz), out, [scratch((half, rows2), F32)],
        [*parts, give_one], nz * rows2 * half,
    )


def sums_body(n, *refs):
    pieces, panels, out, left = refs[:n], refs[n:-2], refs[-2], refs[-1]
    p, _, c = place()
    rows = pieces[0].shape[1] // 2
    depth, half = left.shape[1] // 2, panels[0].shape[1]
    for s in range(n):
        left[:, block(p ^ s, rows)] = pieces[s][:, :rows]
        left[:, pl.ds(pl.multiple_of(depth + (p ^ s) * rows, rows), rows)] = pieces[s][:, rows:]
    for k in range(len(panels) // 2):
        ours, got = panels[2 * k : 2 * k + 2]
        near = dot(left[...], ours[...])
        far = dot(left[:, :depth], got[depth:, :]) + dot(left[:, depth:], got[:depth, :])
        out[:, block(2 * k + c, half)] = near.astype(BF)
        out[:, block(2 * k + 1 - c, half)] = far.astype(BF)


def sums(pieces, panels):
    n, (low, _) = len(pieces), pieces[0].shape
    deep, half = panels[0].shape
    return call(
        functools.partial(sums_body, n), [sds((low, len(panels) * half), BF)], [scratch((low, deep), BF)],
        [*pieces, *panels], 2 * low * deep * half * len(panels),
    )[0]


def top_body(n, *refs):
    mine, theirs = refs[:n], refs[n : 2 * n]
    start, top, top_t, one, two = refs[2 * n : 2 * n + 5]
    corner, inverse_top, rest, own_t, cross = refs[2 * n + 5 :]
    p, _, c = place()
    low, width = mine[0].shape[0], own_t.shape[1]
    for s in range(n):
        for source, t in ((mine[s], c), (theirs[s], 1 - c)):
            rows = block(t * n + (p ^ s), low)
            own_t[rows, :] = source[:, :width]
            cross[rows, :] = source[:, width:]
    own = own_t[...].T
    corner[...] = (one[...].astype(F32) - own.astype(F32)).astype(BF)
    inverse_top[...] = (dot(own, top[...]) - start[...] - cross[...].astype(F32)).astype(BF)
    rest[...] = (
        two[...].astype(F32) - dot(top_t[...], inverse_top[...]) + dot(cross[...].T, top[...])
    )


def top_parts(mine, theirs, start, top, top_t, one, two):
    n, shape = len(mine), top.shape
    out = [sds(shape, BF), sds(shape, BF), sds(shape, F32)]
    return call(
        functools.partial(top_body, n), out, [scratch(shape, BF)] * 2,
        [*mine, *theirs, start, top, top_t, one, two], 6 * shape[0] ** 3,
    )


def last_body(n, *refs):
    mine, theirs, rest, out, tail_t = refs[:n], refs[n : 2 * n], *refs[2 * n :]
    p, _, c = place()
    low = mine[0].shape[0]
    for s in range(n):
        for source, t in ((mine[s], c), (theirs[s], 1 - c)):
            tail_t[block(t * n + (p ^ s), low), :] = source[...]
    out[...] = (rest[...] + tail_t[...].T.astype(F32)).astype(BF)


def last_part(mine, theirs, rest):
    return call(
        functools.partial(last_body, len(mine)), [sds(rest.shape, BF)], [scratch(rest.shape, BF)],
        [*mine, *theirs, rest], 2 * math.prod(rest.shape),
    )[0]


def finish_body(keep_one, keep_two, got, top, flags, inverse_one, inverse_two, value):
    _, _, c = place()
    half = keep_one.shape[1]
    inverse_one[:, block(c, half)] = keep_one[...]
    inverse_one[:, block(1 - c, half)] = got[:, :half].astype(BF)
    value[:, block(c, half)] = keep_two[...]
    value[:, block(1 - c, half)] = got[:, half:]
    lower = -(value[...] + dot(inverse_one[...], top[...]))
    inverse_two[...] = kept_rows(flags[...], lower).astype(BF)


def finish(keep_one, keep_two, got, top, flags):
    shape = (keep_one.shape[0], top.shape[1])
    return call(
        finish_body, [sds(shape, BF)] * 2, [scratch(shape, F32)],
        [keep_one, keep_two, got, top, flags], 2 * shape[0] * top.shape[0] * shape[1],
    )


def on_device(
    n, m, known_inverse, pattern, panel_one, panel_two, panel_top, structure, diag_one, diag_two
):
    row_count = known_inverse.shape[0]
    col_groups = known_inverse.shape[1]
    piece_rows = known_inverse.shape[3]
    nz = m // 2
    block_rows = row_count // BLK
    piece_blocks = piece_rows // BLK
    send = lambda x, axis, size, s: lax.ppermute(x, axis, [(k, k ^ s) for k in range(size)])
    swap = lambda x: send(x, "pcol", m, 1)
    over_z = lambda x, s: send(x, "pcol", m, 2 * s)
    over_p = lambda x, s: send(x, "prow", n, s)

    across = lambda x, s: lax.ppermute(
        x, ("prow", "pcol"),
        [(k * m + j, (k ^ s) * m + (j ^ 1)) for k in range(n) for j in range(m)],
    )

    flags = structure.reshape(1, piece_rows)
    own_one, other_one = split(panel_one)
    near_one = [own_one] + [over_p(own_one, s) for s in range(1, n)]
    far_one = [across(other_one, s) for s in range(n)]
    masked_two = keep(flags, panel_two)
    mine_two = pick(masked_two, swap(masked_two))
    near_two = [mine_two] + [over_p(mine_two, s) for s in range(1, n)]

    shaped = known_inverse.reshape(block_rows, BLK, col_groups, piece_blocks, BLK)
    flag_table = pattern.reshape(block_rows, 1, col_groups, piece_blocks, 1)
    masked = jnp.where(flag_table > 0, shaped, jnp.zeros_like(shaped)).reshape(
        row_count, col_groups * piece_rows
    )
    others = swap(masked)
    start, top_t = start_parts(diag_one, panel_top)

    def exchange(stay, leave):
        got, s = over_z(leave, 1), 2
        while s < nz:
            stay, leave = fold(stay, got)
            got, s = over_z(leave, s), 2 * s
        return [stay, got]

    def spread(pieces):
        return [pieces[0]] + [over_p(pieces[s], s) for s in range(1, n)]

    def total(here):
        s = 1
        while s < nz:
            here = add(here, over_z(here, s))
            s *= 2
        got = [here] + [over_p(here, s) for s in range(1, n)]
        return got, [swap(got[s]) for s in range(n)]

    *parts_one, rows_one = product(masked, others, near_one, far_one, nz)
    parts_one = exchange(*parts_one)
    *parts_two, rows_two = product(masked, others, near_two, [], nz)
    parts_two = exchange(*parts_two)
    panels = [rows_one, swap(rows_one), rows_two, swap(rows_two)]
    keep_one, give_one, *pieces_one = first_turn(parts_one, n)
    pieces_one = spread(pieces_one)
    keep_two, give, *pieces_two = second_turn(parts_two, give_one, n)
    pieces_two = spread(pieces_two)
    sums_one = sums(pieces_one, panels)
    sums_two = sums(pieces_two, panels[2:])
    corner_one, inverse_top, rest = top_parts(
        *total(sums_one), start, panel_top, top_t, diag_one, diag_two
    )
    corner_two = last_part(*total(sums_two), rest)
    inverse_one, inverse_two = finish(keep_one, keep_two, swap(give), panel_top, flags)
    return inverse_one, corner_one, inverse_top, inverse_two, corner_two


def solution(mesh):
    in_specs = (
        P("prow", None, "pcol", None),
        P("prow", None, "pcol", None),
        P(("prow", "pcol"), None),
        P(("prow", "pcol"), None),
        P(),
        P(("prow", "pcol")),
        P(),
        P(),
    )
    out_specs = (P(("prow", "pcol"), None), P(), P(), P(("prow", "pcol"), None), P())
    n, m = mesh.shape["prow"], mesh.shape["pcol"]

    def body(*args):
        return on_device(n, m, *args)

    return jax.shard_map(body, mesh=mesh, in_specs=in_specs, out_specs=out_specs, check_vma=False)
```

```python
import functools
import math

import jax
import jax.numpy as jnp
from jax import lax
from jax.experimental import pallas as pl
from jax.experimental.pallas import tpu as pltpu
from jax.sharding import PartitionSpec as P


BLK = 128
BF = jnp.bfloat16
F32 = jnp.float32

VMEM = pl.BlockSpec(memory_space=pltpu.VMEM)


def sds(shape, dtype):
    return jax.ShapeDtypeStruct(shape, dtype)


def scratch(shape, dtype):
    return pltpu.VMEM(shape, dtype)


def call(body, out, temps, args, flops):
    size = lambda a: math.prod(a.shape) * jnp.dtype(a.dtype).itemsize
    held = sum(size(a) for a in (*args, *out))
    room = held + sum(size(t) for t in temps) + sum(2 * size(t) for t in out)
    return pl.pallas_call(
        body,
        out_shape=out,
        in_specs=[VMEM] * len(args),
        out_specs=[VMEM] * len(out),
        scratch_shapes=temps,
        cost_estimate=pl.CostEstimate(flops=flops, bytes_accessed=held, transcendentals=0),
        compiler_params=pltpu.CompilerParams(vmem_limit_bytes=room + (4 << 20)),
    )(*args)


def tree(parts):
    while len(parts) > 1:
        parts = [parts[k] + parts[k + 1] for k in range(0, len(parts), 2)]
    return parts[0]


def dot(a, b):
    return jnp.dot(a, b, preferred_element_type=F32)


def place():
    j = lax.axis_index("pcol")
    return lax.axis_index("prow"), j >> 1, j & 1


def block(index, size):
    return pl.ds(pl.multiple_of(index * size, size), size)


def pick_body(own, got, out):
    _, _, c = place()
    rows, half = own.shape[0], out.shape[1]
    out[:rows, :] = own[:, block(c, half)]
    out[rows:, :] = got[:, block(c, half)]


def pick(own, got):
    rows, width = own.shape
    return call(pick_body, [sds((2 * rows, width // 2), BF)], [], [own, got], 0)[0]


def kept_rows(flags, values):
    rows = values.shape[0]
    mask = jnp.broadcast_to(flags.astype(F32), (rows, rows)).T > 0
    mask = jnp.concatenate([mask.astype(F32)] * (values.shape[1] // rows), axis=1)
    return jnp.where(mask > 0, values, jnp.zeros_like(values))


def keep_body(flags, values, out):
    out[...] = kept_rows(flags[...], values[...].astype(F32)).astype(BF)


def keep(flags, values):
    return call(keep_body, [sds(values.shape, BF)], [], [flags, values], values.size)[0]


def add_body(one, two, out):
    out[...] = (one[...].astype(F32) + two[...].astype(F32)).astype(out.dtype)


def add(one, two):
    return call(add_body, [sds(one.shape, BF)], [], [one, two], one.size)[0]


def start_body(one, top, start, top_t):
    start[...] = dot(one[...], top[...])
    top_t[...] = top[...].T


def start_parts(one, top):
    out = [sds(top.shape, F32), sds(top.shape, BF)]
    return call(start_body, out, [], [one, top], 2 * top.shape[0] ** 3)


def sequence(nz):
    if nz == 1:
        return [0]
    stay = [2 * k for k in sequence(nz // 2)]
    return stay + [k ^ 1 for k in stay]


def product_body(n, nz, mine, theirs, *refs):
    q, (stay, leave, rhs) = refs[:n], refs[n:]
    p, z, c = place()
    depth = rhs.shape[0] // 2
    rows = depth // n
    for s in range(n):
        rhs[block(p ^ s, rows), :] = q[s][:rows, :]
        rhs[pl.ds(pl.multiple_of(depth + (p ^ s) * rows, rows), rows), :] = q[s][rows:, :]
    order = sequence(nz)
    for k in range(nz // 2, nz):
        emit(leave, k - nz // 2, order[k], z, c, rows, mine, theirs, rhs)
    for k in range(nz // 2):
        emit(stay, k, order[k], z, c, rows, mine, theirs, rhs)


def emit(out, k, offset, z, c, rows, mine, theirs, rhs):
    depth = rhs.shape[0] // 2
    span = block(z ^ offset, 2 * rows)
    value = dot(mine[span, :], rhs[:depth, :]) + dot(theirs[span, :], rhs[depth:, :])
    for t in range(2):
        out[block(2 * k + (c ^ t), rows), :] = value[t * rows : (t + 1) * rows].astype(out.dtype)


def product(mine, theirs, q, nz):
    n, (rows, half) = len(q), q[0].shape
    depth = mine.shape[1]
    shape = (nz // 2 * rows, half)
    out = [sds(shape, F32), sds(shape, BF), sds((2 * depth, half), BF)]
    return call(
        functools.partial(product_body, n, nz), out, [],
        [mine, theirs, *q], 4 * mine.shape[0] * depth * half,
    )


def fold_body(held, got, stay, leave):
    rows = stay.shape[0]
    stay[...] = held[:rows] + got[:rows].astype(F32)
    leave[...] = (held[rows:] + got[rows:].astype(F32)).astype(BF)


def fold(held, got):
    shape = (held.shape[0] // 2, held.shape[1])
    return call(fold_body, [sds(shape, F32), sds(shape, BF)], [], [held, got], 2 * held.size)


def first_body(n, nz, *refs):
    parts = refs[:nz]
    keep, give, outs, turned = refs[nz], refs[nz + 1], refs[nz + 2 : nz + 2 + n], refs[nz + 2 + n]
    p, _, _ = place()
    rows = keep.shape[0]
    inverse = -tree([parts[s][...].astype(F32) for s in range(nz)])
    keep[...] = inverse[:rows].astype(BF)
    give[...] = inverse[rows:].astype(BF)
    turned[...] = inverse.T
    for s in range(n):
        outs[s][...] = turned[block(p ^ s, outs[s].shape[0]), :].astype(BF)


def second_body(n, nz, *refs):
    parts, give_one = refs[:nz], refs[nz]
    keep, give, outs, turned = refs[nz + 1], refs[nz + 2], refs[nz + 3 : nz + 3 + n], refs[nz + 3 + n]
    p, _, _ = place()
    rows, half = keep.shape
    value = tree([parts[s][...].astype(F32) for s in range(nz)])
    keep[...] = value[:rows]
    give[:, :half] = give_one[...].astype(F32)
    give[:, half:] = value[rows:]
    turned[...] = value.T
    for s in range(n):
        outs[s][...] = turned[block(p ^ s, outs[s].shape[0]), :].astype(BF)


def first_turn(parts, n):
    nz, (rows2, half) = len(parts), parts[0].shape
    out = [sds((rows2 // 2, half), BF)] * 2 + [sds((half // n, rows2), BF)] * n
    return call(
        functools.partial(first_body, n, nz), out, [scratch((half, rows2), F32)],
        parts, nz * rows2 * half,
    )


def second_turn(parts, give_one, n):
    nz, (rows2, half) = len(parts), parts[0].shape
    out = [sds((rows2 // 2, half), F32), sds((rows2 // 2, 2 * half), F32)]
    out += [sds((half // n, rows2), BF)] * n
    return call(
        functools.partial(second_body, n, nz), out, [scratch((half, rows2), F32)],
        [*parts, give_one], nz * rows2 * half,
    )


def sums_body(n, *refs):
    pieces, panels, out, left = refs[:n], refs[n:-2], refs[-2], refs[-1]
    p, _, c = place()
    rows = pieces[0].shape[1] // 2
    depth, half = left.shape[1] // 2, panels[0].shape[1]
    for s in range(n):
        left[:, block(p ^ s, rows)] = pieces[s][:, :rows]
        left[:, pl.ds(pl.multiple_of(depth + (p ^ s) * rows, rows), rows)] = pieces[s][:, rows:]
    for k in range(len(panels) // 2):
        ours, got = panels[2 * k : 2 * k + 2]
        near = dot(left[...], ours[...])
        far = dot(left[:, :depth], got[depth:, :]) + dot(left[:, depth:], got[:depth, :])
        out[:, block(2 * k + c, half)] = near.astype(BF)
        out[:, block(2 * k + 1 - c, half)] = far.astype(BF)


def sums(pieces, panels):
    n, (low, _) = len(pieces), pieces[0].shape
    deep, half = panels[0].shape
    return call(
        functools.partial(sums_body, n), [sds((low, len(panels) * half), BF)], [scratch((low, deep), BF)],
        [*pieces, *panels], 2 * low * deep * half * len(panels),
    )[0]


def stack_body(n, *refs):
    p, _, _ = place()
    for s in range(n):
        refs[n][block(p ^ s, refs[s].shape[0]), :] = refs[s][...]


def stack(parts):
    n, (low, width) = len(parts), parts[0].shape
    return call(functools.partial(stack_body, n), [sds((n * low, width), BF)], [], parts, 0)[0]


def top_body(mine, theirs, start, top, top_t, one, two, corner, inverse_top, rest, own_t, cross):
    _, _, c = place()
    half, width = mine.shape[0], own_t.shape[1]
    for source, t in ((mine, c), (theirs, 1 - c)):
        own_t[block(t, half), :] = source[:, :width]
        cross[block(t, half), :] = source[:, width:]
    own = own_t[...].T
    corner[...] = (one[...].astype(F32) - own.astype(F32)).astype(BF)
    inverse_top[...] = (dot(own, top[...]) - start[...] - cross[...].astype(F32)).astype(BF)
    rest[...] = (
        two[...].astype(F32) - dot(top_t[...], inverse_top[...]) + dot(cross[...].T, top[...])
    )


def top_parts(mine, theirs, start, top, top_t, one, two):
    shape = top.shape
    out = [sds(shape, BF), sds(shape, BF), sds(shape, F32)]
    return call(
        top_body, out, [scratch(shape, BF)] * 2,
        [mine, theirs, start, top, top_t, one, two], 6 * shape[0] ** 3,
    )


def last_body(mine, theirs, rest, out, tail_t):
    _, _, c = place()
    half = mine.shape[0]
    for source, t in ((mine, c), (theirs, 1 - c)):
        tail_t[block(t, half), :] = source[...]
    out[...] = (rest[...] + tail_t[...].T.astype(F32)).astype(BF)


def last_part(mine, theirs, rest):
    return call(
        last_body, [sds(rest.shape, BF)], [scratch(rest.shape, BF)],
        [mine, theirs, rest], 2 * math.prod(rest.shape),
    )[0]


def finish_body(keep_one, keep_two, got, top, flags, inverse_one, inverse_two, value):
    _, _, c = place()
    half = keep_one.shape[1]
    inverse_one[:, block(c, half)] = keep_one[...]
    inverse_one[:, block(1 - c, half)] = got[:, :half].astype(BF)
    value[:, block(c, half)] = keep_two[...]
    value[:, block(1 - c, half)] = got[:, half:]
    lower = -(value[...] + dot(inverse_one[...], top[...]))
    inverse_two[...] = kept_rows(flags[...], lower).astype(BF)


def finish(keep_one, keep_two, got, top, flags):
    shape = (keep_one.shape[0], top.shape[1])
    return call(
        finish_body, [sds(shape, BF)] * 2, [scratch(shape, F32)],
        [keep_one, keep_two, got, top, flags], 2 * shape[0] * top.shape[0] * shape[1],
    )


def on_device(
    n, m, known_inverse, pattern, panel_one, panel_two, panel_top, structure, diag_one, diag_two
):
    row_count = known_inverse.shape[0]
    col_groups = known_inverse.shape[1]
    piece_rows = known_inverse.shape[3]
    nz = m // 2
    block_rows = row_count // BLK
    piece_blocks = piece_rows // BLK
    send = lambda x, axis, size, s: lax.ppermute(x, axis, [(k, k ^ s) for k in range(size)])
    swap = lambda x: send(x, "pcol", m, 1)
    over_z = lambda x, s: send(x, "pcol", m, 2 * s)
    over_p = lambda x, s: send(x, "prow", n, s)

    flags = structure.reshape(1, piece_rows)
    gather = lambda x: [x] + [over_p(x, s) for s in range(1, n)]
    mine_one = pick(panel_one, swap(panel_one))
    gathered_one = gather(mine_one)
    masked_two = keep(flags, panel_two)
    mine_two = pick(masked_two, swap(masked_two))
    gathered_two = gather(mine_two)

    shaped = known_inverse.reshape(block_rows, BLK, col_groups, piece_blocks, BLK)
    flag_table = pattern.reshape(block_rows, 1, col_groups, piece_blocks, 1)
    masked = jnp.where(flag_table > 0, shaped, jnp.zeros_like(shaped)).reshape(
        row_count, col_groups * piece_rows
    )
    others = swap(masked)
    start, top_t = start_parts(diag_one, panel_top)

    def exchange(stay, leave):
        got, s = over_z(leave, 1), 2
        while s < nz:
            stay, leave = fold(stay, got)
            got, s = over_z(leave, s), 2 * s
        return [stay, got]

    def spread(pieces):
        return [pieces[0]] + [over_p(pieces[s], s) for s in range(1, n)]

    def total(here):
        s = 1
        while s < nz:
            here = add(here, over_z(here, s))
            s *= 2
        held = stack([here] + [over_p(here, s) for s in range(1, n)])
        return held, swap(held)

    *parts_one, rows_one = product(masked, others, gathered_one, nz)
    parts_one = exchange(*parts_one)
    *parts_two, rows_two = product(masked, others, gathered_two, nz)
    parts_two = exchange(*parts_two)
    panels = [rows_one, swap(rows_one), rows_two, swap(rows_two)]
    keep_one, give_one, *pieces_one = first_turn(parts_one, n)
    pieces_one = spread(pieces_one)
    keep_two, give, *pieces_two = second_turn(parts_two, give_one, n)
    pieces_two = spread(pieces_two)
    sums_one = sums(pieces_one, panels)
    sums_two = sums(pieces_two, panels[2:])
    corner_one, inverse_top, rest = top_parts(
        *total(sums_one), start, panel_top, top_t, diag_one, diag_two
    )
    corner_two = last_part(*total(sums_two), rest)
    inverse_one, inverse_two = finish(keep_one, keep_two, swap(give), panel_top, flags)
    return inverse_one, corner_one, inverse_top, inverse_two, corner_two


def solution(mesh):
    in_specs = (
        P("prow", None, "pcol", None),
        P("prow", None, "pcol", None),
        P(("prow", "pcol"), None),
        P(("prow", "pcol"), None),
        P(),
        P(("prow", "pcol")),
        P(),
        P(),
    )
    out_specs = (P(("prow", "pcol"), None), P(), P(), P(("prow", "pcol"), None), P())
    n, m = mesh.shape["prow"], mesh.shape["pcol"]

    def body(*args):
        return on_device(n, m, *args)

    return jax.shard_map(body, mesh=mesh, in_specs=in_specs, out_specs=out_specs, check_vma=False)
```

```python
import functools
import math

import jax
import jax.numpy as jnp
from jax import lax
from jax.experimental import pallas as pl
from jax.experimental.pallas import tpu as pltpu
from jax.sharding import PartitionSpec as P


BLK = 128
BF = jnp.bfloat16
F32 = jnp.float32

VMEM = pl.BlockSpec(memory_space=pltpu.VMEM)


def sds(shape, dtype):
    return jax.ShapeDtypeStruct(shape, dtype)


def scratch(shape, dtype):
    return pltpu.VMEM(shape, dtype)


def call(body, out, temps, args, flops):
    size = lambda a: math.prod(a.shape) * jnp.dtype(a.dtype).itemsize
    held = sum(size(a) for a in (*args, *out))
    room = held + sum(size(t) for t in temps) + sum(2 * size(t) for t in out)
    return pl.pallas_call(
        body,
        out_shape=out,
        in_specs=[VMEM] * len(args),
        out_specs=[VMEM] * len(out),
        scratch_shapes=temps,
        cost_estimate=pl.CostEstimate(flops=flops, bytes_accessed=held, transcendentals=0),
        compiler_params=pltpu.CompilerParams(vmem_limit_bytes=room + (4 << 20)),
    )(*args)


def total_of(parts):
    return sum(part[...].astype(F32) for part in parts)


def dot(a, b):
    return jnp.dot(a, b, preferred_element_type=F32)


def place():
    j = lax.axis_index("pcol")
    return lax.axis_index("prow"), j >> 1, j & 1


def block(index, size):
    return pl.ds(pl.multiple_of(index * size, size), size)


def pick_body(own, got, out):
    _, _, c = place()
    rows, half = own.shape[0], out.shape[1]
    out[:rows, :] = own[:, block(c, half)]
    out[rows:, :] = got[:, block(c, half)]


def pick(own, got):
    rows, width = own.shape
    return call(pick_body, [sds((2 * rows, width // 2), BF)], [], [own, got], 0)[0]


def kept_rows(flags, values):
    rows = values.shape[0]
    mask = jnp.broadcast_to(flags.astype(F32), (rows, rows)).T > 0
    mask = jnp.concatenate([mask.astype(F32)] * (values.shape[1] // rows), axis=1)
    return jnp.where(mask > 0, values, jnp.zeros_like(values))


def keep_body(flags, values, out):
    out[...] = kept_rows(flags[...], values[...].astype(F32)).astype(BF)


def keep(flags, values):
    return call(keep_body, [sds(values.shape, BF)], [], [flags, values], values.size)[0]


def add_body(one, two, out):
    out[...] = (one[...].astype(F32) + two[...].astype(F32)).astype(out.dtype)


def add(one, two, kind=BF):
    return call(add_body, [sds(one.shape, kind)], [], [one, two], one.size)[0]


def start_body(one, top, start, top_t):
    start[...] = dot(one[...], top[...])
    top_t[...] = top[...].T


def start_parts(one, top):
    out = [sds(top.shape, F32), sds(top.shape, BF)]
    return call(start_body, out, [], [one, top], 2 * top.shape[0] ** 3)


def sequence(nz):
    if nz == 1:
        return [0]
    stay = [2 * k for k in sequence(nz // 2)]
    return stay + [k ^ 1 for k in stay]


def product_body(n, nz, mine, theirs, *refs):
    q, (*outs, rhs) = refs[:n], refs[n:]
    p, z, c = place()
    depth = rhs.shape[0] // 2
    rows = depth // n
    for s in range(n):
        rhs[block(p ^ s, rows), :] = q[s][:rows, :]
        rhs[pl.ds(pl.multiple_of(depth + (p ^ s) * rows, rows), rows), :] = q[s][rows:, :]
    order, size = sequence(nz), nz // 4
    for k in reversed(range(nz)):
        emit(outs[k // size], k % size, order[k], z, c, rows, mine, theirs, rhs)


def emit(out, k, offset, z, c, rows, mine, theirs, rhs):
    depth = rhs.shape[0] // 2
    span = block(z ^ offset, 2 * rows)
    value = dot(mine[span, :], rhs[:depth, :]) + dot(theirs[span, :], rhs[depth:, :])
    for t in range(2):
        out[block(2 * k + (c ^ t), rows), :] = value[t * rows : (t + 1) * rows].astype(out.dtype)


def product(mine, theirs, q, nz):
    n, (rows, half) = len(q), q[0].shape
    depth = mine.shape[1]
    shape = (nz // 4 * rows, half)
    out = [sds(shape, F32)] * 2 + [sds(shape, BF)] * 2 + [sds((2 * depth, half), BF)]
    return call(
        functools.partial(product_body, n, nz), out, [],
        [mine, theirs, *q], 4 * mine.shape[0] * depth * half,
    )


def first_body(n, nz, *refs):
    parts = refs[:nz]
    keep, give, outs, turned = refs[nz], refs[nz + 1], refs[nz + 2 : nz + 2 + n], refs[nz + 2 + n]
    p, _, _ = place()
    rows = keep.shape[0]
    inverse = -total_of(parts)
    keep[...] = inverse[:rows].astype(BF)
    give[...] = inverse[rows:].astype(BF)
    turned[...] = inverse.T
    for s in range(n):
        outs[s][...] = turned[block(p ^ s, outs[s].shape[0]), :].astype(BF)


def second_body(n, nz, *refs):
    parts, give_one = refs[:nz], refs[nz]
    keep, give, outs, turned = refs[nz + 1], refs[nz + 2], refs[nz + 3 : nz + 3 + n], refs[nz + 3 + n]
    p, _, _ = place()
    rows, half = keep.shape
    value = total_of(parts)
    keep[...] = value[:rows]
    give[:, :half] = give_one[...].astype(F32)
    give[:, half:] = value[rows:]
    turned[...] = value.T
    for s in range(n):
        outs[s][...] = turned[block(p ^ s, outs[s].shape[0]), :].astype(BF)


def first_turn(parts, n):
    nz, (rows2, half) = len(parts), parts[0].shape
    out = [sds((rows2 // 2, half), BF)] * 2 + [sds((half // n, rows2), BF)] * n
    return call(
        functools.partial(first_body, n, nz), out, [scratch((half, rows2), F32)],
        parts, nz * rows2 * half,
    )


def second_turn(parts, give_one, n):
    nz, (rows2, half) = len(parts), parts[0].shape
    out = [sds((rows2 // 2, half), F32), sds((rows2 // 2, 2 * half), F32)]
    out += [sds((half // n, rows2), BF)] * n
    return call(
        functools.partial(second_body, n, nz), out, [scratch((half, rows2), F32)],
        [*parts, give_one], nz * rows2 * half,
    )


def sums_body(n, *refs):
    pieces, panels, out, left = refs[:n], refs[n:-2], refs[-2], refs[-1]
    p, _, c = place()
    rows = pieces[0].shape[1] // 2
    depth, half = left.shape[1] // 2, panels[0].shape[1]
    for s in range(n):
        left[:, block(p ^ s, rows)] = pieces[s][:, :rows]
        left[:, pl.ds(pl.multiple_of(depth + (p ^ s) * rows, rows), rows)] = pieces[s][:, rows:]
    for k in range(len(panels) // 2):
        ours, got = panels[2 * k : 2 * k + 2]
        near = dot(left[...], ours[...])
        far = dot(left[:, :depth], got[depth:, :]) + dot(left[:, depth:], got[:depth, :])
        out[:, block(2 * k + c, half)] = near.astype(BF)
        out[:, block(2 * k + 1 - c, half)] = far.astype(BF)


def sums(pieces, panels):
    n, (low, _) = len(pieces), pieces[0].shape
    deep, half = panels[0].shape
    return call(
        functools.partial(sums_body, n), [sds((low, len(panels) * half), BF)], [scratch((low, deep), BF)],
        [*pieces, *panels], 2 * low * deep * half * len(panels),
    )[0]


def stack_body(n, *refs):
    p, _, _ = place()
    for s in range(n):
        refs[n][block(p ^ s, refs[s].shape[0]), :] = refs[s][...]


def stack(parts):
    n, (low, width) = len(parts), parts[0].shape
    return call(functools.partial(stack_body, n), [sds((n * low, width), BF)], [], parts, 0)[0]


def top_body(mine, theirs, start, top, top_t, one, two, corner, inverse_top, rest, own_t, cross):
    _, _, c = place()
    half, width = mine.shape[0], own_t.shape[1]
    for source, t in ((mine, c), (theirs, 1 - c)):
        own_t[block(t, half), :] = source[:, :width]
        cross[block(t, half), :] = source[:, width:]
    own = own_t[...].T
    corner[...] = (one[...].astype(F32) - own.astype(F32)).astype(BF)
    inverse_top[...] = (dot(own, top[...]) - start[...] - cross[...].astype(F32)).astype(BF)
    rest[...] = (
        two[...].astype(F32) - dot(top_t[...], inverse_top[...]) + dot(cross[...].T, top[...])
    )


def top_parts(mine, theirs, start, top, top_t, one, two):
    shape = top.shape
    out = [sds(shape, BF), sds(shape, BF), sds(shape, F32)]
    return call(
        top_body, out, [scratch(shape, BF)] * 2,
        [mine, theirs, start, top, top_t, one, two], 6 * shape[0] ** 3,
    )


def last_body(mine, theirs, rest, out, tail_t):
    _, _, c = place()
    half = mine.shape[0]
    for source, t in ((mine, c), (theirs, 1 - c)):
        tail_t[block(t, half), :] = source[...]
    out[...] = (rest[...] + tail_t[...].T.astype(F32)).astype(BF)


def last_part(mine, theirs, rest):
    return call(
        last_body, [sds(rest.shape, BF)], [scratch(rest.shape, BF)],
        [mine, theirs, rest], 2 * math.prod(rest.shape),
    )[0]


def finish_body(keep_one, keep_two, got, top, flags, inverse_one, inverse_two, value):
    _, _, c = place()
    half = keep_one.shape[1]
    inverse_one[:, block(c, half)] = keep_one[...]
    inverse_one[:, block(1 - c, half)] = got[:, :half].astype(BF)
    value[:, block(c, half)] = keep_two[...]
    value[:, block(1 - c, half)] = got[:, half:]
    lower = -(value[...] + dot(inverse_one[...], top[...]))
    inverse_two[...] = kept_rows(flags[...], lower).astype(BF)


def finish(keep_one, keep_two, got, top, flags):
    shape = (keep_one.shape[0], top.shape[1])
    return call(
        finish_body, [sds(shape, BF)] * 2, [scratch(shape, F32)],
        [keep_one, keep_two, got, top, flags], 2 * shape[0] * top.shape[0] * shape[1],
    )


def on_device(
    n, m, known_inverse, pattern, panel_one, panel_two, panel_top, structure, diag_one, diag_two
):
    row_count = known_inverse.shape[0]
    col_groups = known_inverse.shape[1]
    piece_rows = known_inverse.shape[3]
    nz = m // 2
    block_rows = row_count // BLK
    piece_blocks = piece_rows // BLK
    send = lambda x, axis, size, s: lax.ppermute(x, axis, [(k, k ^ s) for k in range(size)])
    swap = lambda x: send(x, "pcol", m, 1)
    over_z = lambda x, s: send(x, "pcol", m, 2 * s)
    over_p = lambda x, s: send(x, "prow", n, s)

    flags = structure.reshape(1, piece_rows)
    gather = lambda x: [x] + [over_p(x, s) for s in range(1, n)]
    mine_one = pick(panel_one, swap(panel_one))
    gathered_one = gather(mine_one)
    masked_two = keep(flags, panel_two)
    mine_two = pick(masked_two, swap(masked_two))
    gathered_two = gather(mine_two)

    shaped = known_inverse.reshape(block_rows, BLK, col_groups, piece_blocks, BLK)
    flag_table = pattern.reshape(block_rows, 1, col_groups, piece_blocks, 1)
    kept = jnp.broadcast_to(flag_table > 0, shaped.shape)
    masked = jnp.where(kept, shaped, jnp.zeros_like(shaped)).reshape(
        row_count, col_groups * piece_rows
    )
    others = swap(masked)
    start, top_t = start_parts(diag_one, panel_top)

    def exchange(keep_held, go_held, keep_leave, go_leave):
        s, count = 1, nz // 4
        while True:
            go_got = over_z(go_leave, s)
            keep_got = over_z(keep_leave, s)
            s *= 2
            leave = add(go_held, go_got)
            if count == 1:
                return [keep_held, keep_got, over_z(leave, s)]
            held = add(keep_held, keep_got, F32)
            keep_held, go_held = jnp.split(held, 2)
            keep_leave, go_leave = jnp.split(leave, 2)
            count //= 2

    def spread(pieces):
        return [pieces[0]] + [over_p(pieces[s], s) for s in range(1, n)]

    def total(here):
        s = 1
        while s < nz:
            here = add(here, over_z(here, s))
            s *= 2
        held = stack([here] + [over_p(here, s) for s in range(1, n)])
        return held, swap(held)

    *parts_one, rows_one = product(masked, others, gathered_one, nz)
    parts_one = exchange(*parts_one)
    *parts_two, rows_two = product(masked, others, gathered_two, nz)
    parts_two = exchange(*parts_two)
    panels = [rows_one, swap(rows_one), rows_two, swap(rows_two)]
    keep_one, give_one, *pieces_one = first_turn(parts_one, n)
    pieces_one = spread(pieces_one)
    keep_two, give, *pieces_two = second_turn(parts_two, give_one, n)
    pieces_two = spread(pieces_two)
    sums_one = sums(pieces_one, panels)
    sums_two = sums(pieces_two, panels[2:])
    corner_one, inverse_top, rest = top_parts(
        *total(sums_one), start, panel_top, top_t, diag_one, diag_two
    )
    corner_two = last_part(*total(sums_two), rest)
    inverse_one, inverse_two = finish(keep_one, keep_two, swap(give), panel_top, flags)
    return inverse_one, corner_one, inverse_top, inverse_two, corner_two


def solution(mesh):
    in_specs = (
        P("prow", None, "pcol", None),
        P("prow", None, "pcol", None),
        P(("prow", "pcol"), None),
        P(("prow", "pcol"), None),
        P(),
        P(("prow", "pcol")),
        P(),
        P(),
    )
    out_specs = (P(("prow", "pcol"), None), P(), P(), P(("prow", "pcol"), None), P())
    n, m = mesh.shape["prow"], mesh.shape["pcol"]

    def body(*args):
        return on_device(n, m, *args)

    return jax.shard_map(body, mesh=mesh, in_specs=in_specs, out_specs=out_specs, check_vma=False)
```

```python
import functools
import math

import jax
import jax.numpy as jnp
from jax import lax
from jax.experimental import pallas as pl
from jax.experimental.pallas import tpu as pltpu
from jax.sharding import PartitionSpec as P


BLK = 128
BF = jnp.bfloat16
F32 = jnp.float32

VMEM = pl.BlockSpec(memory_space=pltpu.VMEM)


def sds(shape, dtype):
    return jax.ShapeDtypeStruct(shape, dtype)


def scratch(shape, dtype):
    return pltpu.VMEM(shape, dtype)


def call(body, out, temps, args, flops):
    size = lambda a: math.prod(a.shape) * jnp.dtype(a.dtype).itemsize
    held = sum(size(a) for a in (*args, *out))
    room = held + sum(size(t) for t in temps) + sum(2 * size(t) for t in out)
    return pl.pallas_call(
        body,
        out_shape=out,
        in_specs=[VMEM] * len(args),
        out_specs=[VMEM] * len(out),
        scratch_shapes=temps,
        cost_estimate=pl.CostEstimate(flops=flops, bytes_accessed=held, transcendentals=0),
        compiler_params=pltpu.CompilerParams(vmem_limit_bytes=room + (4 << 20)),
    )(*args)


def total_of(parts):
    return sum(part[...].astype(F32) for part in parts)


def dot(a, b):
    return jnp.dot(a, b, preferred_element_type=F32)


def place():
    j = lax.axis_index("pcol")
    return lax.axis_index("prow"), j >> 1, j & 1


def block(index, size):
    return pl.ds(pl.multiple_of(index * size, size), size)


def pick_body(own, got, out):
    _, _, c = place()
    rows, half = own.shape[0], out.shape[1]
    out[:rows, :] = own[:, block(c, half)]
    out[rows:, :] = got[:, block(c, half)]


def pick(own, got):
    rows, width = own.shape
    return call(pick_body, [sds((2 * rows, width // 2), BF)], [], [own, got], 0)[0]


def kept_rows(flags, values):
    rows = values.shape[0]
    mask = jnp.broadcast_to(flags.astype(F32), (rows, rows)).T > 0
    mask = jnp.concatenate([mask.astype(F32)] * (values.shape[1] // rows), axis=1)
    return jnp.where(mask > 0, values, jnp.zeros_like(values))


def keep_body(flags, values, out):
    out[...] = kept_rows(flags[...], values[...].astype(F32)).astype(BF)


def keep(flags, values):
    return call(keep_body, [sds(values.shape, BF)], [], [flags, values], values.size)[0]


def tree_body(*refs):
    parts, out = [ref[...].astype(F32) for ref in refs[:-1]], refs[-1]
    while len(parts) > 1:
        parts = [parts[k] + parts[k + 1] for k in range(0, len(parts), 2)]
    out[...] = parts[0].astype(BF)


def tree(parts):
    one = parts[0]
    return call(tree_body, [sds(one.shape, BF)], [], parts, len(parts) * one.size)[0]


def add_body(one, two, out):
    out[...] = (one[...].astype(F32) + two[...].astype(F32)).astype(out.dtype)


def add(one, two, kind=BF):
    return call(add_body, [sds(one.shape, kind)], [], [one, two], one.size)[0]


def start_body(one, top, start, top_t):
    start[...] = dot(one[...], top[...])
    top_t[...] = top[...].T


def start_parts(one, top):
    out = [sds(top.shape, F32), sds(top.shape, BF)]
    return call(start_body, out, [], [one, top], 2 * top.shape[0] ** 3)


def sequence(nz):
    if nz == 1:
        return [0]
    stay = [2 * k for k in sequence(nz // 2)]
    return stay + [k ^ 1 for k in stay]


def product_body(n, nz, mine, theirs, *refs):
    q, (*outs, rhs) = refs[:n], refs[n:]
    p, z, c = place()
    depth = rhs.shape[0] // 2
    rows = depth // n
    for s in range(n):
        rhs[block(p ^ s, rows), :] = q[s][:rows, :]
        rhs[pl.ds(pl.multiple_of(depth + (p ^ s) * rows, rows), rows), :] = q[s][rows:, :]
    order, size = sequence(nz), nz // 4
    for k in reversed(range(nz)):
        emit(outs[k // size], k % size, order[k], z, c, rows, mine, theirs, rhs)


def emit(out, k, offset, z, c, rows, mine, theirs, rhs):
    depth = rhs.shape[0] // 2
    span = block(z ^ offset, 2 * rows)
    value = dot(mine[span, :], rhs[:depth, :]) + dot(theirs[span, :], rhs[depth:, :])
    for t in range(2):
        out[block(2 * k + (c ^ t), rows), :] = value[t * rows : (t + 1) * rows].astype(out.dtype)


def product(mine, theirs, q, nz):
    n, (rows, half) = len(q), q[0].shape
    depth = mine.shape[1]
    shape = (nz // 4 * rows, half)
    out = [sds(shape, F32)] * 2 + [sds(shape, BF)] * 2 + [sds((2 * depth, half), BF)]
    return call(
        functools.partial(product_body, n, nz), out, [],
        [mine, theirs, *q], 4 * mine.shape[0] * depth * half,
    )


def first_body(n, nz, *refs):
    parts = refs[:nz]
    keep, give, outs, turned = refs[nz], refs[nz + 1], refs[nz + 2 : nz + 2 + n], refs[nz + 2 + n]
    p, _, _ = place()
    rows = keep.shape[0]
    inverse = -total_of(parts)
    keep[...] = inverse[:rows].astype(BF)
    give[...] = inverse[rows:].astype(BF)
    turned[...] = inverse.T
    for s in range(n):
        outs[s][...] = turned[block(p ^ s, outs[s].shape[0]), :].astype(BF)


def second_body(n, nz, *refs):
    parts, give_one = refs[:nz], refs[nz]
    keep, give, outs, turned = refs[nz + 1], refs[nz + 2], refs[nz + 3 : nz + 3 + n], refs[nz + 3 + n]
    p, _, _ = place()
    rows, half = keep.shape
    value = total_of(parts)
    keep[...] = value[:rows]
    give[:, :half] = give_one[...].astype(F32)
    give[:, half:] = value[rows:]
    turned[...] = value.T
    for s in range(n):
        outs[s][...] = turned[block(p ^ s, outs[s].shape[0]), :].astype(BF)


def first_turn(parts, n):
    nz, (rows2, half) = len(parts), parts[0].shape
    out = [sds((rows2 // 2, half), BF)] * 2 + [sds((half // n, rows2), BF)] * n
    return call(
        functools.partial(first_body, n, nz), out, [scratch((half, rows2), F32)],
        parts, nz * rows2 * half,
    )


def second_turn(parts, give_one, n):
    nz, (rows2, half) = len(parts), parts[0].shape
    out = [sds((rows2 // 2, half), F32), sds((rows2 // 2, 2 * half), F32)]
    out += [sds((half // n, rows2), BF)] * n
    return call(
        functools.partial(second_body, n, nz), out, [scratch((half, rows2), F32)],
        [*parts, give_one], nz * rows2 * half,
    )


def sums_body(n, *refs):
    pieces, panels, out, left = refs[:n], refs[n:-2], refs[-2], refs[-1]
    p, _, c = place()
    rows = pieces[0].shape[1] // 2
    depth, half = left.shape[1] // 2, panels[0].shape[1]
    for s in range(n):
        left[:, block(p ^ s, rows)] = pieces[s][:, :rows]
        left[:, pl.ds(pl.multiple_of(depth + (p ^ s) * rows, rows), rows)] = pieces[s][:, rows:]
    for k in range(len(panels) // 2):
        ours, got = panels[2 * k : 2 * k + 2]
        near = dot(left[...], ours[...])
        far = dot(left[:, :depth], got[depth:, :]) + dot(left[:, depth:], got[:depth, :])
        out[:, block(2 * k + c, half)] = near.astype(BF)
        out[:, block(2 * k + 1 - c, half)] = far.astype(BF)


def sums(pieces, panels):
    n, (low, _) = len(pieces), pieces[0].shape
    deep, half = panels[0].shape
    return call(
        functools.partial(sums_body, n), [sds((low, len(panels) * half), BF)], [scratch((low, deep), BF)],
        [*pieces, *panels], 2 * low * deep * half * len(panels),
    )[0]


def stack_body(n, *refs):
    p, _, _ = place()
    for s in range(n):
        refs[n][block(p ^ s, refs[s].shape[0]), :] = refs[s][...]


def stack(parts):
    n, (low, width) = len(parts), parts[0].shape
    return call(functools.partial(stack_body, n), [sds((n * low, width), BF)], [], parts, 0)[0]


def top_body(mine, theirs, start, top, top_t, one, two, corner, inverse_top, rest, own_t, cross):
    _, _, c = place()
    half, width = mine.shape[0], own_t.shape[1]
    for source, t in ((mine, c), (theirs, 1 - c)):
        own_t[block(t, half), :] = source[:, :width]
        cross[block(t, half), :] = source[:, width:]
    own = own_t[...].T
    corner[...] = (one[...].astype(F32) - own.astype(F32)).astype(BF)
    inverse_top[...] = (dot(own, top[...]) - start[...] - cross[...].astype(F32)).astype(BF)
    rest[...] = (
        two[...].astype(F32) - dot(top_t[...], inverse_top[...]) + dot(cross[...].T, top[...])
    )


def top_parts(mine, theirs, start, top, top_t, one, two):
    shape = top.shape
    out = [sds(shape, BF), sds(shape, BF), sds(shape, F32)]
    return call(
        top_body, out, [scratch(shape, BF)] * 2,
        [mine, theirs, start, top, top_t, one, two], 6 * shape[0] ** 3,
    )


def last_body(mine, theirs, rest, out, tail_t):
    _, _, c = place()
    half = mine.shape[0]
    for source, t in ((mine, c), (theirs, 1 - c)):
        tail_t[block(t, half), :] = source[...]
    out[...] = (rest[...] + tail_t[...].T.astype(F32)).astype(BF)


def last_part(mine, theirs, rest):
    return call(
        last_body, [sds(rest.shape, BF)], [scratch(rest.shape, BF)],
        [mine, theirs, rest], 2 * math.prod(rest.shape),
    )[0]


def finish_body(keep_one, keep_two, got, top, flags, inverse_one, inverse_two, value):
    _, _, c = place()
    half = keep_one.shape[1]
    inverse_one[:, block(c, half)] = keep_one[...]
    inverse_one[:, block(1 - c, half)] = got[:, :half].astype(BF)
    value[:, block(c, half)] = keep_two[...]
    value[:, block(1 - c, half)] = got[:, half:]
    lower = -(value[...] + dot(inverse_one[...], top[...]))
    inverse_two[...] = kept_rows(flags[...], lower).astype(BF)


def finish(keep_one, keep_two, got, top, flags):
    shape = (keep_one.shape[0], top.shape[1])
    return call(
        finish_body, [sds(shape, BF)] * 2, [scratch(shape, F32)],
        [keep_one, keep_two, got, top, flags], 2 * shape[0] * top.shape[0] * shape[1],
    )


def on_device(
    n, m, known_inverse, pattern, panel_one, panel_two, panel_top, structure, diag_one, diag_two
):
    row_count = known_inverse.shape[0]
    col_groups = known_inverse.shape[1]
    piece_rows = known_inverse.shape[3]
    nz = m // 2
    block_rows = row_count // BLK
    piece_blocks = piece_rows // BLK
    send = lambda x, axis, size, s: lax.ppermute(x, axis, [(k, k ^ s) for k in range(size)])
    swap = lambda x: send(x, "pcol", m, 1)
    over_z = lambda x, s: send(x, "pcol", m, 2 * s)
    over_p = lambda x, s: send(x, "prow", n, s)

    flags = structure.reshape(1, piece_rows)
    gather = lambda x: [x] + [over_p(x, s) for s in range(1, n)]
    mine_one = pick(panel_one, swap(panel_one))
    gathered_one = gather(mine_one)
    masked_two = keep(flags, panel_two)
    mine_two = pick(masked_two, swap(masked_two))
    gathered_two = gather(mine_two)

    shaped = known_inverse.reshape(block_rows, BLK, col_groups, piece_blocks, BLK)
    flag_table = pattern.reshape(block_rows, 1, col_groups, piece_blocks, 1)
    masked = jnp.where(flag_table > 0, shaped, jnp.zeros_like(shaped)).reshape(
        row_count, col_groups * piece_rows
    )
    others = swap(masked)
    start, top_t = start_parts(diag_one, panel_top)

    def exchange(keep_held, go_held, keep_leave, go_leave):
        s, count = 1, nz // 4
        while True:
            go_got = over_z(go_leave, s)
            keep_got = over_z(keep_leave, s)
            s *= 2
            leave = add(go_held, go_got)
            if count == 1:
                return [keep_held, keep_got, over_z(leave, s)]
            held = add(keep_held, keep_got, F32)
            keep_held, go_held = jnp.split(held, 2)
            keep_leave, go_leave = jnp.split(leave, 2)
            count //= 2

    def spread(pieces):
        return [pieces[0]] + [over_p(pieces[s], s) for s in range(1, n)]

    def doubled(here):
        for k in range(nz.bit_length() - 1):
            here = add(here, over_z(here, 2**k))
        return here

    def spread_out(here):
        held = stack([here] + [over_p(here, s) for s in range(1, n)])
        return held, swap(held)

    *parts_one, rows_one = product(masked, others, gathered_one, nz)
    parts_one = exchange(*parts_one)
    *parts_two, rows_two = product(masked, others, gathered_two, nz)
    parts_two = exchange(*parts_two)
    panels = [rows_one, swap(rows_one), rows_two, swap(rows_two)]
    keep_one, give_one, *pieces_one = first_turn(parts_one, n)
    pieces_one = spread(pieces_one)
    keep_two, give, *pieces_two = second_turn(parts_two, give_one, n)
    pieces_two = spread(pieces_two)
    sums_one = sums(pieces_one, panels)
    sums_two = sums(pieces_two, panels[2:])
    corner_one, inverse_top, rest = top_parts(
        *spread_out(doubled(sums_one)), start, panel_top, top_t, diag_one, diag_two
    )
    sums_two = tree([sums_two] + [over_z(sums_two, s) for s in range(1, nz)])
    corner_two = last_part(*spread_out(sums_two), rest)
    inverse_one, inverse_two = finish(keep_one, keep_two, swap(give), panel_top, flags)
    return inverse_one, corner_one, inverse_top, inverse_two, corner_two


def solution(mesh):
    in_specs = (
        P("prow", None, "pcol", None),
        P("prow", None, "pcol", None),
        P(("prow", "pcol"), None),
        P(("prow", "pcol"), None),
        P(),
        P(("prow", "pcol")),
        P(),
        P(),
    )
    out_specs = (P(("prow", "pcol"), None), P(), P(), P(("prow", "pcol"), None), P())
    n, m = mesh.shape["prow"], mesh.shape["pcol"]

    def body(*args):
        return on_device(n, m, *args)

    return jax.shard_map(body, mesh=mesh, in_specs=in_specs, out_specs=out_specs, check_vma=False)
```

```python
import functools
import math

import jax
import jax.numpy as jnp
from jax import lax
from jax.experimental import pallas as pl
from jax.experimental.pallas import tpu as pltpu
from jax.sharding import PartitionSpec as P


BLK = 128
BF = jnp.bfloat16
F32 = jnp.float32

VMEM = pl.BlockSpec(memory_space=pltpu.VMEM)


def sds(shape, dtype):
    return jax.ShapeDtypeStruct(shape, dtype)


def scratch(shape, dtype):
    return pltpu.VMEM(shape, dtype)


def call(body, out, temps, args, flops):
    size = lambda a: math.prod(a.shape) * jnp.dtype(a.dtype).itemsize
    held = sum(size(a) for a in (*args, *out))
    room = held + sum(size(t) for t in temps) + sum(2 * size(t) for t in out)
    return pl.pallas_call(
        body,
        out_shape=out,
        in_specs=[VMEM] * len(args),
        out_specs=[VMEM] * len(out),
        scratch_shapes=temps,
        cost_estimate=pl.CostEstimate(flops=flops, bytes_accessed=held, transcendentals=0),
        compiler_params=pltpu.CompilerParams(vmem_limit_bytes=room + (4 << 20)),
    )(*args)


def total_of(parts):
    return sum(part[...].astype(F32) for part in parts)


def dot(a, b):
    return jnp.dot(a, b, preferred_element_type=F32)


def place():
    j = lax.axis_index("pcol")
    return lax.axis_index("prow"), j >> 1, j & 1


def block(index, size):
    return pl.ds(pl.multiple_of(index * size, size), size)


def pick_body(own, got, out):
    _, _, c = place()
    rows, half = own.shape[0], out.shape[1]
    out[:rows, :] = own[:, block(c, half)]
    out[rows:, :] = got[:, block(c, half)]


def pick(own, got):
    rows, width = own.shape
    return call(pick_body, [sds((2 * rows, width // 2), BF)], [], [own, got], 0)[0]


def kept_rows(flags, values):
    rows = values.shape[0]
    mask = jnp.broadcast_to(flags.astype(F32), (rows, rows)).T > 0
    mask = jnp.concatenate([mask.astype(F32)] * (values.shape[1] // rows), axis=1)
    return jnp.where(mask > 0, values, jnp.zeros_like(values))


def keep_body(flags, values, out):
    out[...] = kept_rows(flags[...], values[...].astype(F32)).astype(BF)


def keep(flags, values):
    return call(keep_body, [sds(values.shape, BF)], [], [flags, values], values.size)[0]


def tree_body(*refs):
    parts, out = [ref[...].astype(F32) for ref in refs[:-1]], refs[-1]
    while len(parts) > 1:
        parts = [parts[k] + parts[k + 1] for k in range(0, len(parts), 2)]
    out[...] = parts[0].astype(BF)


def tree(parts):
    one = parts[0]
    return call(tree_body, [sds(one.shape, BF)], [], parts, len(parts) * one.size)[0]


def add_body(one, two, out):
    out[...] = (one[...].astype(F32) + two[...].astype(F32)).astype(out.dtype)


def add(one, two, kind=BF):
    return call(add_body, [sds(one.shape, kind)], [], [one, two], one.size)[0]


def start_body(one, top, start, top_t):
    start[...] = dot(one[...], top[...])
    top_t[...] = top[...].T


def start_parts(one, top):
    out = [sds(top.shape, F32), sds(top.shape, BF)]
    return call(start_body, out, [], [one, top], 2 * top.shape[0] ** 3)


def sequence(nz):
    if nz == 1:
        return [0]
    stay = [2 * k for k in sequence(nz // 2)]
    return stay + [k ^ 1 for k in stay]


def lead_body(n, nz, mine, theirs, *refs):
    q, (out, rhs) = refs[:n], refs[n:]
    p, z, c = place()
    depth = rhs.shape[0] // 2
    rows = depth // n
    for s in range(n):
        rhs[block(p ^ s, rows), :] = q[s][:rows, :]
        rhs[pl.ds(pl.multiple_of(depth + (p ^ s) * rows, rows), rows), :] = q[s][rows:, :]
    order, size = sequence(nz), nz // 4
    for k in range(size):
        emit(out, k, order[3 * size + k], z, c, rows, mine, theirs, rhs)


def product_body(n, nz, mine, theirs, rhs, *outs):
    _, z, c = place()
    rows = rhs.shape[0] // (2 * n)
    order, size = sequence(nz), nz // 4
    for k in range(3 * size):
        emit(outs[k // size], k % size, order[k], z, c, rows, mine, theirs, rhs)


def emit(out, k, offset, z, c, rows, mine, theirs, rhs):
    depth = rhs.shape[0] // 2
    span = block(z ^ offset, 2 * rows)
    value = dot(mine[span, :], rhs[:depth, :]) + dot(theirs[span, :], rhs[depth:, :])
    for t in range(2):
        out[block(2 * k + (c ^ t), rows), :] = value[t * rows : (t + 1) * rows].astype(out.dtype)


def lead(mine, theirs, q, nz):
    n, (rows, half) = len(q), q[0].shape
    depth = mine.shape[1]
    shape = (nz // 4 * rows, half)
    return call(
        functools.partial(lead_body, n, nz), [sds(shape, BF), sds((2 * depth, half), BF)], [],
        [mine, theirs, *q], mine.shape[0] * depth * half,
    )


def product(mine, theirs, rhs, n, nz):
    depth, half = mine.shape[1], rhs.shape[1]
    shape = (mine.shape[0] // 4, half)
    return call(
        functools.partial(product_body, n, nz), [sds(shape, F32)] * 2 + [sds(shape, BF)], [],
        [mine, theirs, rhs], 3 * mine.shape[0] * depth * half,
    )


def first_body(n, nz, *refs):
    parts = refs[:nz]
    keep, give, outs, turned = refs[nz], refs[nz + 1], refs[nz + 2 : nz + 2 + n], refs[nz + 2 + n]
    p, _, _ = place()
    rows = keep.shape[0]
    inverse = -total_of(parts)
    keep[...] = inverse[:rows].astype(BF)
    give[...] = inverse[rows:].astype(BF)
    turned[...] = inverse.T
    for s in range(n):
        outs[s][...] = turned[block(p ^ s, outs[s].shape[0]), :].astype(BF)


def second_body(n, nz, *refs):
    parts, give_one = refs[:nz], refs[nz]
    keep, give, outs, turned = refs[nz + 1], refs[nz + 2], refs[nz + 3 : nz + 3 + n], refs[nz + 3 + n]
    p, _, _ = place()
    rows, half = keep.shape
    value = total_of(parts)
    keep[...] = value[:rows]
    give[:, :half] = give_one[...].astype(F32)
    give[:, half:] = value[rows:]
    turned[...] = value.T
    for s in range(n):
        outs[s][...] = turned[block(p ^ s, outs[s].shape[0]), :].astype(BF)


def first_turn(parts, n):
    nz, (rows2, half) = len(parts), parts[0].shape
    out = [sds((rows2 // 2, half), BF)] * 2 + [sds((half // n, rows2), BF)] * n
    return call(
        functools.partial(first_body, n, nz), out, [scratch((half, rows2), F32)],
        parts, nz * rows2 * half,
    )


def second_turn(parts, give_one, n):
    nz, (rows2, half) = len(parts), parts[0].shape
    out = [sds((rows2 // 2, half), F32), sds((rows2 // 2, 2 * half), F32)]
    out += [sds((half // n, rows2), BF)] * n
    return call(
        functools.partial(second_body, n, nz), out, [scratch((half, rows2), F32)],
        [*parts, give_one], nz * rows2 * half,
    )


def sums_body(n, *refs):
    pieces, panels, out, left = refs[:n], refs[n:-2], refs[-2], refs[-1]
    p, _, c = place()
    rows = pieces[0].shape[1] // 2
    depth, half = left.shape[1] // 2, panels[0].shape[1]
    for s in range(n):
        left[:, block(p ^ s, rows)] = pieces[s][:, :rows]
        left[:, pl.ds(pl.multiple_of(depth + (p ^ s) * rows, rows), rows)] = pieces[s][:, rows:]
    for k in range(len(panels) // 2):
        ours, got = panels[2 * k : 2 * k + 2]
        near = dot(left[...], ours[...])
        far = dot(left[:, :depth], got[depth:, :]) + dot(left[:, depth:], got[:depth, :])
        out[:, block(2 * k + c, half)] = near.astype(BF)
        out[:, block(2 * k + 1 - c, half)] = far.astype(BF)


def sums(pieces, panels):
    n, (low, _) = len(pieces), pieces[0].shape
    deep, half = panels[0].shape
    return call(
        functools.partial(sums_body, n), [sds((low, len(panels) * half), BF)], [scratch((low, deep), BF)],
        [*pieces, *panels], 2 * low * deep * half * len(panels),
    )[0]


def stack_body(n, *refs):
    p, _, _ = place()
    for s in range(n):
        refs[n][block(p ^ s, refs[s].shape[0]), :] = refs[s][...]


def stack(parts):
    n, (low, width) = len(parts), parts[0].shape
    return call(functools.partial(stack_body, n), [sds((n * low, width), BF)], [], parts, 0)[0]


def top_body(mine, theirs, start, top, top_t, one, two, corner, inverse_top, rest, own_t, cross):
    _, _, c = place()
    half, width = mine.shape[0], own_t.shape[1]
    for source, t in ((mine, c), (theirs, 1 - c)):
        own_t[block(t, half), :] = source[:, :width]
        cross[block(t, half), :] = source[:, width:]
    own = own_t[...].T
    corner[...] = (one[...].astype(F32) - own.astype(F32)).astype(BF)
    inverse_top[...] = (dot(own, top[...]) - start[...] - cross[...].astype(F32)).astype(BF)
    rest[...] = (
        two[...].astype(F32) - dot(top_t[...], inverse_top[...]) + dot(cross[...].T, top[...])
    )


def top_parts(mine, theirs, start, top, top_t, one, two):
    shape = top.shape
    out = [sds(shape, BF), sds(shape, BF), sds(shape, F32)]
    return call(
        top_body, out, [scratch(shape, BF)] * 2,
        [mine, theirs, start, top, top_t, one, two], 6 * shape[0] ** 3,
    )


def last_body(mine, theirs, rest, out, tail_t):
    _, _, c = place()
    half = mine.shape[0]
    for source, t in ((mine, c), (theirs, 1 - c)):
        tail_t[block(t, half), :] = source[...]
    out[...] = (rest[...] + tail_t[...].T.astype(F32)).astype(BF)


def last_part(mine, theirs, rest):
    return call(
        last_body, [sds(rest.shape, BF)], [scratch(rest.shape, BF)],
        [mine, theirs, rest], 2 * math.prod(rest.shape),
    )[0]


def finish_body(keep_one, keep_two, got, top, flags, inverse_one, inverse_two, value):
    _, _, c = place()
    half = keep_one.shape[1]
    inverse_one[:, block(c, half)] = keep_one[...]
    inverse_one[:, block(1 - c, half)] = got[:, :half].astype(BF)
    value[:, block(c, half)] = keep_two[...]
    value[:, block(1 - c, half)] = got[:, half:]
    lower = -(value[...] + dot(inverse_one[...], top[...]))
    inverse_two[...] = kept_rows(flags[...], lower).astype(BF)


def finish(keep_one, keep_two, got, top, flags):
    shape = (keep_one.shape[0], top.shape[1])
    return call(
        finish_body, [sds(shape, BF)] * 2, [scratch(shape, F32)],
        [keep_one, keep_two, got, top, flags], 2 * shape[0] * top.shape[0] * shape[1],
    )


def on_device(
    n, m, known_inverse, pattern, panel_one, panel_two, panel_top, structure, diag_one, diag_two
):
    row_count = known_inverse.shape[0]
    col_groups = known_inverse.shape[1]
    piece_rows = known_inverse.shape[3]
    nz = m // 2
    block_rows = row_count // BLK
    piece_blocks = piece_rows // BLK
    send = lambda x, axis, size, s: lax.ppermute(x, axis, [(k, k ^ s) for k in range(size)])
    swap = lambda x: send(x, "pcol", m, 1)
    over_z = lambda x, s: send(x, "pcol", m, 2 * s)
    over_p = lambda x, s: send(x, "prow", n, s)

    flags = structure.reshape(1, piece_rows)
    gather = lambda x: [x] + [over_p(x, s) for s in range(1, n)]
    mine_one = pick(panel_one, swap(panel_one))
    gathered_one = gather(mine_one)
    masked_two = keep(flags, panel_two)
    mine_two = pick(masked_two, swap(masked_two))
    gathered_two = gather(mine_two)

    shaped = known_inverse.reshape(block_rows, BLK, col_groups, piece_blocks, BLK)
    flag_table = pattern.reshape(block_rows, 1, col_groups, piece_blocks, 1)
    masked = jnp.where(flag_table > 0, shaped, jnp.zeros_like(shaped)).reshape(
        row_count, col_groups * piece_rows
    )
    others = swap(masked)
    start, top_t = start_parts(diag_one, panel_top)

    def exchange(keep_held, go_held, keep_leave, go_leave):
        s, count = 1, nz // 4
        while True:
            go_got = over_z(go_leave, s)
            keep_got = over_z(keep_leave, s)
            s *= 2
            leave = add(go_held, go_got)
            if count == 1:
                return [keep_held, keep_got, over_z(leave, s)]
            held = add(keep_held, keep_got, F32)
            keep_held, go_held = jnp.split(held, 2)
            keep_leave, go_leave = jnp.split(leave, 2)
            count //= 2

    def spread(pieces):
        return [pieces[0]] + [over_p(pieces[s], s) for s in range(1, n)]

    def doubled(here):
        for k in range(nz.bit_length() - 1):
            here = add(here, over_z(here, 2**k))
        return here

    def spread_out(here):
        held = stack([here] + [over_p(here, s) for s in range(1, n)])
        return held, swap(held)

    go_one, rows_one = lead(masked, others, gathered_one, nz)
    rest_one = product(masked, others, rows_one, n, nz)
    parts_one = exchange(*rest_one, go_one)
    go_two, rows_two = lead(masked, others, gathered_two, nz)
    rest_two = product(masked, others, rows_two, n, nz)
    parts_two = exchange(*rest_two, go_two)
    panels = [rows_one, swap(rows_one), rows_two, swap(rows_two)]
    keep_one, give_one, *pieces_one = first_turn(parts_one, n)
    pieces_one = spread(pieces_one)
    keep_two, give, *pieces_two = second_turn(parts_two, give_one, n)
    pieces_two = spread(pieces_two)
    sums_one = sums(pieces_one, panels)
    sums_two = sums(pieces_two, panels[2:])
    corner_one, inverse_top, rest = top_parts(
        *spread_out(doubled(sums_one)), start, panel_top, top_t, diag_one, diag_two
    )
    sums_two = tree([sums_two] + [over_z(sums_two, s) for s in range(1, nz)])
    corner_two = last_part(*spread_out(sums_two), rest)
    inverse_one, inverse_two = finish(keep_one, keep_two, swap(give), panel_top, flags)
    return inverse_one, corner_one, inverse_top, inverse_two, corner_two


def solution(mesh):
    in_specs = (
        P("prow", None, "pcol", None),
        P("prow", None, "pcol", None),
        P(("prow", "pcol"), None),
        P(("prow", "pcol"), None),
        P(),
        P(("prow", "pcol")),
        P(),
        P(),
    )
    out_specs = (P(("prow", "pcol"), None), P(), P(), P(("prow", "pcol"), None), P())
    n, m = mesh.shape["prow"], mesh.shape["pcol"]

    def body(*args):
        return on_device(n, m, *args)

    return jax.shard_map(body, mesh=mesh, in_specs=in_specs, out_specs=out_specs, check_vma=False)
```
